256 devices in a mesh: gx: 16 (over x, y), gy: 16 (over z, core).
Axes of the slice: x: 4, y: 4, z: 8, core: 2. Of those that a mesh axis runs over, the one named last changes fastest.
Arguments:
- potential: float32 [1024, 512, 128], P('gx', 'gy'), may hold values from -6 to 6
- coefficient: float32 [1024, 512, 128], P('gx', 'gy'), may hold values from -1 to 1
- shock_switch: int32 [1024, 512, 128], P('gx', 'gy'), may hold values 0 or 1
- x_factors: float32 [2, 1024, 512, 128], P(None, 'gx', 'gy'), may hold values from 0.3 to 1, as said below
- y_factors: float32 [2, 1024, 512, 128], P(None, 'gx', 'gy'), may hold values from 0.3 to 1, as said below
- wing_lead: int32 [512], P('gy'), may hold values from 0 to 255
- wing_chord: int32 [512], P('gy'), may hold values from 256 to 512
- panel_mode: int32 [1024, 512], P('gx', 'gy'), may hold values from 0 to 1
Outputs:
- correction: float32 [1024, 512, 128], P('gx', 'gy')
- station_loads: float32 [2, 512], P(None, 'gy')
The draws below stay inside these ranges and needn't reach their ends.
Inputs may be any that keep to these rules, and one draw needn't show every extreme that they name: `x_factors`: each ratio lies strictly between 0 and 1. `y_factors`: each ratio lies strictly between 0 and 1.
All inputs are finite; a program needn't handle non-finite values. No bound on the sum of `shock_switch` on one device may be relied on, other than what follows from the above.
Results may differ from the reference program's by a relative error of at most 0.0003.
Values sent between devices are 32-bit elements; how exact they have to be, the bound alone decides.
A program may use at most 64 MiB of HBM per device.

```python
import math
import jax
import jax.numpy as jnp
from jax import lax

NZ = 128
MODES = 2
NX = 1024
NY = 512


def decay_ratios(key, sweep_direction, slow_share):
    complete_extent = (2, NX, NY, NZ)
    sweep_length = complete_extent[sweep_direction]
    line_shape = list(complete_extent)
    line_shape[sweep_direction] = 1
    line_shape = tuple(line_shape)
    random_key_list = jax.random.split(key, 5)
    slow_line = jax.random.uniform(random_key_list[0], line_shape) < slow_share
    slow_rate = jnp.exp(jax.random.uniform(random_key_list[1], line_shape, minval=math.log(0.1), maxval=math.log(0.6))) / sweep_length
    fast_rate = 1.0 / jax.random.uniform(random_key_list[2], line_shape, minval=20.0, maxval=50.0)
    damping_factor = jnp.where(slow_line, slow_rate, fast_rate)
    surface_jaggedness = jnp.exp(jax.random.uniform(random_key_list[3], complete_extent, minval=math.log(0.5), maxval=math.log(2.0)))
    impulse_locations = jax.random.randint(random_key_list[4], (3,), 0, sweep_length)
    grid_location = lax.broadcasted_iota(jnp.int32, complete_extent, sweep_direction)
    impulse_values = jnp.ones(complete_extent, jnp.float32)
    for impulse_index in range(3):
        impulse_values = impulse_values * jnp.where(grid_location == impulse_locations[impulse_index], 0.7, 1.0)
    return (jnp.exp(-damping_factor * surface_jaggedness) * impulse_values).astype(jnp.float32)


def draw_x_factors(key, part):
    slow_share = 0.5
    return decay_ratios(jax.random.fold_in(key, 11), 1, slow_share)


def draw_y_factors(key, part):
    slow_share = 0.5
    return decay_ratios(jax.random.fold_in(key, 23), 2, slow_share)


def with_ends(result, own_key, smallest, top_value):
    longest = result.shape.index(max(result.shape))
    spots = []
    for shift in (0, 1):
        where = [jax.random.randint(jax.random.fold_in(own_key, axis), (), 0, length) for axis, length in enumerate(result.shape)]
        where[longest] = (where[longest] + shift) % result.shape[longest]
        spots.append(tuple(where))
    return result.at[spots[0]].set(smallest).at[spots[1]].set(top_value)


def block_scale(own_key, extent, cuts, low, largest):
    def one(dim, parts):
        draws = jax.random.uniform(jax.random.fold_in(jax.random.fold_in(own_key, 6), dim), (parts,), jnp.float32, low / len(cuts), largest / len(cuts))
        return jnp.repeat(jnp.exp(draws), extent[dim] // parts).reshape((-1,) + (1,) * (len(extent) - dim - 1))

    loudness = one(*cuts[0])
    for cut in cuts[1:]:
        loudness = loudness * one(*cut)
    return loudness


def noise(own_key, shape, deviation, reach, shards=(), kind=jnp.bfloat16):
    array = jax.random.normal(own_key, shape, jnp.float32) * deviation
    if len(shards) > 0:
        array = block_scale(own_key, shape, shards, -0.22, 0.18) * array
    return jnp.clip(array, min=-reach, max=reach).astype(kind)


def setup_inputs(seed: int = 0) -> dict:
    arg_keys = jax.random.split(jax.random.key(seed), 9)
    return {
        "potential": noise(arg_keys[0], (NX, NY, NZ), 1.0, 6.0, ((0, 16), (1, 16)), jnp.float32),
        "coefficient": jnp.clip(jax.random.uniform(arg_keys[1], (NX, NY, NZ), jnp.float32, -1.0, 1.0) * block_scale(arg_keys[1], (NX, NY, NZ), ((0, 16), (1, 16)), -0.4, 0.0), -1.0, 1.0),
        "shock_switch": with_ends((jax.random.randint(arg_keys[2], (NX, NY, NZ), 0, 4) < 1).astype(jnp.int32), jax.random.fold_in(arg_keys[2], 1), 0, 1),
        "x_factors": draw_x_factors(jax.random.fold_in(arg_keys[8], 71), 0),
        "y_factors": draw_y_factors(jax.random.fold_in(arg_keys[8], 71), 0),
        "wing_lead": with_ends(jax.random.randint(arg_keys[5], (NY,), 0, NX // 4), jax.random.fold_in(arg_keys[5], 1), 0, (NX // 4) - 1).astype(jnp.int32),
        "wing_chord": with_ends(jax.random.randint(arg_keys[6], (NY,), NX // 4, NX // 2 + 1), jax.random.fold_in(arg_keys[6], 1), NX // 4, (NX // 2 + 1) - 1).astype(jnp.int32),
        "panel_mode": with_ends(jax.random.randint(arg_keys[7], (NX, NY), 0, MODES), jax.random.fold_in(arg_keys[7], 1), 0, MODES - 1).astype(jnp.int32),
    }


def residual_of(potential, coefficient, shock_switch):
    padded = jnp.pad(potential, ((2, 2), (2, 2), (1, 1)))
    center = padded[2:-2, 2:-2, 1:-1]
    central = padded[3:-1, 2:-2, 1:-1] - 2.0 * center + padded[1:-3, 2:-2, 1:-1]
    upwind = center - 2.0 * padded[1:-3, 2:-2, 1:-1] + padded[:-4, 2:-2, 1:-1]
    second_x = jnp.where(shock_switch == 1, upwind, central)
    second_y = padded[2:-2, 3:-1, 1:-1] - 2.0 * center + padded[2:-2, 1:-3, 1:-1]
    second_z = padded[2:-2, 2:-2, 2:] - 2.0 * center + padded[2:-2, 2:-2, :-2]
    return coefficient * second_x + second_y + second_z

def ratio_sweep(forcing_input, ratios, sweep_direction, backward_order):
    moved_source = jnp.moveaxis(forcing_input, sweep_direction, 0)
    moved_ratios = jnp.moveaxis(ratios, sweep_direction, 0)

    def advance(carried, element):
        source_cell, multiplier_term = element
        following = multiplier_term * carried + jnp.sqrt(1.0 - multiplier_term * multiplier_term) * source_cell
        return (following, following)
    initial = jnp.zeros(moved_source.shape[1:], jnp.float32)
    final, results = lax.scan(advance, initial, (moved_source, moved_ratios), reverse=backward_order)
    return jnp.moveaxis(results, 0, sweep_direction)

def reference(potential, coefficient, shock_switch, x_factors, y_factors, wing_lead, wing_chord, panel_mode):
    forcing = 0.25 * residual_of(potential, coefficient, shock_switch)
    forward_x = ratio_sweep(forcing, x_factors[0], 0, False)
    backward_x = ratio_sweep(forward_x, x_factors[1], 0, True)
    forward_y = ratio_sweep(backward_x, y_factors[0], 1, False)
    correction = ratio_sweep(forward_y, y_factors[1], 1, True)
    updated = potential + correction
    depth = NZ // 2
    jump_value = updated[:, :, depth] - updated[:, :, depth - 1]
    stream_pos = jnp.arange(NX, dtype=jnp.int32)[:, None]
    onwing = (stream_pos >= wing_lead[None, :]) & (stream_pos < (wing_lead + wing_chord)[None, :])
    weight = 0.5 + 2.5 * stream_pos.astype(jnp.float32) / NX
    scaled = jnp.where(onwing, weight * jump_value, jnp.float32(0.0)) / jnp.sqrt(wing_chord.astype(jnp.float32))[None, :]
    station_loads = jnp.stack([lax.optimization_barrier(jnp.sum(jnp.where(panel_mode == mode_index, scaled, jnp.float32(0.0)), axis=0)) for mode_index in range(MODES)])
    return (correction, station_loads)
```

```python
import functools

import jax
import jax.numpy as jnp
from jax import lax
from jax.experimental import pallas as pl
from jax.experimental.pallas import tpu as pltpu
from jax.sharding import PartitionSpec as P

MODES = 2
MESH = pl.DeviceIdType.MESH
F32 = jnp.float32


def complement(ratio):
    return jnp.sqrt(1.0 - ratio * ratio)


def kernel(nx, ny, I, J, Z, *refs):
    (pot, coef, switch, xf, yf, lead, chord, mode, out, loads,
     p, cf, sw, xr, yr, xq, xs, xg, xo,
     to, tg, tc, yr0, ysc, yr1, ys1, yfw, ycb, ygb, ycc,
     face_hi, face_lo, halo_lo, halo_hi, halo_prev, halo_next, strip,
     xgs, xgr, xos, xor_, xas, xar, ygs, ygr, yos, yor, yas, yar, ls, lr, ya, yb,
     load_sem, halo_send, halo_recv, push_send, push_recv) = refs
    mx = lax.axis_index("gx")
    my = lax.axis_index("gy")
    xrow, yrow = J // nx, I // ny
    U = 8

    barrier = pltpu.get_barrier_semaphore()

    def greet_x(k, _):
        pl.semaphore_signal(barrier, inc=1, device_id=(lax.rem(mx + k, nx), my), device_id_type=MESH)
        return 0

    def greet_y(k, _):
        pl.semaphore_signal(barrier, inc=1, device_id=(mx, lax.rem(my + k, ny)), device_id_type=MESH)
        return 0

    lax.fori_loop(1, nx, greet_x, 0)
    lax.fori_loop(1, ny, greet_y, 0)

    load_p = pltpu.make_async_copy(pot, p.at[pl.ds(2 * J, I * J), :], load_sem.at[0])
    load_x = pltpu.make_async_copy(xf, xr, load_sem.at[1])
    load_c = pltpu.make_async_copy(coef, cf, load_sem.at[2])
    load_s = pltpu.make_async_copy(switch, sw, load_sem.at[3])
    load_y = pltpu.make_async_copy(yf, yr, load_sem.at[4])
    for load in (load_p, load_x, load_c, load_s, load_y):
        load.start()

    def push(src, dst, along_x, slot):
        me, n = (mx, nx) if along_x else (my, ny)

        def body(k, _):
            peer = lax.rem(me + k, n)
            pltpu.make_async_remote_copy(
                src_ref=src.at[peer],
                dst_ref=dst.at[me],
                send_sem=push_send.at[slot],
                recv_sem=push_recv.at[slot],
                device_id=(peer, my) if along_x else (mx, peer),
                device_id_type=MESH,
            ).start()
            return 0

        lax.fori_loop(1, n, body, 0)

    def arrived(dst, slot):
        part = dst.at[pl.ds(0, dst.shape[0] - 1)]
        pltpu.make_async_copy(part, part, push_recv.at[slot]).wait()

    def drained(src, slot):
        part = src.at[pl.ds(0, src.shape[0] - 1)]
        pltpu.make_async_copy(part, part, push_send.at[slot]).wait()

    def at(ref, index, rows):
        return ref[pl.ds(pl.multiple_of(index * rows, 8), rows), :]

    def put(ref, index, rows, value):
        ref[pl.ds(pl.multiple_of(index * rows, 8), rows), :] = value

    def pack(dst, member, value, rows):
        total = value.shape[0]
        strip[0:total, :] = value
        for s in range(total // rows):
            dst[s, member] = strip[s * rows:(s + 1) * rows, :]

    row = lax.broadcasted_iota(jnp.int32, (J, Z), 0)
    lane = lax.broadcasted_iota(jnp.int32, (J, Z), 1)
    row8 = lax.broadcasted_iota(jnp.int32, (8, Z), 0)

    zero_line = jnp.zeros((J, Z), F32)
    p[0:J, :] = zero_line
    p[J:2 * J, :] = zero_line
    p[(I + 2) * J:(I + 3) * J, :] = zero_line
    load_p.wait()
    face_hi[...] = p[pl.ds(2 * J + J - 1, I, stride=J), :]
    face_lo[...] = p[pl.ds(2 * J, I, stride=J), :]

    load_x.wait()

    def gain_forward(c, gain):
        for u in range(U):
            i = c * U + u
            ratio = at(xr, i, J)
            put(xq, i, J, 0.25 * complement(ratio))
            gain = ratio * gain
            put(xg, i, J, gain)
        return gain

    x_gain = lax.fori_loop(0, I // U, gain_forward, jnp.ones((J, Z), F32))

    def gain_backward(c, carry):
        gain, cross = carry
        for u in range(U):
            i = I - 1 - (c * U + u)
            ratio = at(xr, I + i, J)
            scale = complement(ratio)
            put(xs, i, J, scale)
            gain = ratio * gain
            cross = ratio * cross + scale * at(xg, i, J)
            tg[pl.ds(i, J, stride=I), :] = gain
            tc[pl.ds(i, J, stride=I), :] = cross
        return gain, cross

    x_back, x_cross = lax.fori_loop(
        0, I // U, gain_backward, (jnp.ones((J, Z), F32), jnp.zeros((J, Z), F32)))
    pack(xgs, 0, x_gain, xrow)
    pack(xgs, 1, x_back, xrow)
    pack(xgs, 2, x_cross, xrow)

    pl.semaphore_wait(barrier, nx + ny - 2)

    def neighbour(src, dst, slot, device):
        return pltpu.make_async_remote_copy(
            src_ref=src, dst_ref=dst, send_sem=halo_send.at[slot], recv_sem=halo_recv.at[slot],
            device_id=device, device_id_type=MESH)

    left, right = lax.rem(mx + nx - 1, nx), lax.rem(mx + 1, nx)
    down, up = lax.rem(my + ny - 1, ny), lax.rem(my + 1, ny)
    halos = (
        neighbour(pot.at[pl.ds((I - 2) * J, 2 * J), :], halo_prev, 0, (right, my)),
        neighbour(pot.at[pl.ds(0, J), :], halo_next, 1, (left, my)),
        neighbour(face_hi, halo_lo, 2, (mx, up)),
        neighbour(face_lo, halo_hi, 3, (mx, down)),
    )
    for halo in halos:
        halo.start()
    push(xgs, xgr, True, 0)

    load_c.wait()
    load_s.wait()

    def forcing(c, _):
        for u in range(2):
            i = c * 2 + u
            before2, before, center, after = (at(p, i + d, J) for d in range(4))
            second = jnp.where(at(sw, i, J) == 1, center - 2.0 * before + before2,
                               after - 2.0 * center + before)
            span = jnp.where(row == 0, 0.0, pltpu.roll(center, 1, 0)) + jnp.where(
                row == J - 1, 0.0, pltpu.roll(center, J - 1, 0))
            normal = jnp.where(lane == 0, 0.0, pltpu.roll(center, 1, 1)) + jnp.where(
                lane == Z - 1, 0.0, pltpu.roll(center, Z - 1, 1))
            residual = at(cf, i, J) * second + (span - 2.0 * center) + (normal - 2.0 * center)
            put(xo, i, J, at(xq, i, J) * residual)
        return 0

    lax.fori_loop(0, I // 2, forcing, 0)

    for halo in halos:
        halo.wait_recv()

    before = jnp.where(mx == 0, 0.0, halo_prev[J:2 * J, :])
    before2 = jnp.where(mx == 0, 0.0, halo_prev[0:J, :])
    after = jnp.where(mx == nx - 1, 0.0, halo_next[...])
    first = jnp.where(at(sw, 0, J) == 1, before2 - 2.0 * before, before)
    second = jnp.where(at(sw, 1, J) == 1, before, 0.0)
    last = jnp.where(at(sw, I - 1, J) == 1, 0.0, after)
    for i, term in ((0, first), (1, second), (I - 1, last)):
        put(xo, i, J, at(xo, i, J) + at(xq, i, J) * (at(cf, i, J) * term))
    low = jnp.logical_and(row8 == 0, my > 0)
    high = jnp.logical_and(row8 == 7, my < ny - 1)

    def sweep_forward(c, carry):
        head, body, tail = carry
        low8 = at(halo_lo, c, U)
        high8 = at(halo_hi, c, U)
        for u in range(U):
            base = pl.multiple_of((c * U + u) * J, 8)
            r = xr[pl.ds(base, J), :]
            f = xo[pl.ds(base, J), :]
            q0 = xq[pl.ds(base, 8), :]
            q3 = xq[pl.ds(base + J - 8, 8), :]
            head = r[0:8] * head + (f[0:8] + q0 * jnp.where(low, low8[u:u + 1], 0.0))
            body = r[8:J - 8] * body + f[8:J - 8]
            tail = r[J - 8:] * tail + (f[J - 8:] + q3 * jnp.where(high, high8[u:u + 1], 0.0))
            xo[pl.ds(base, 8), :] = head
            xo[pl.ds(base + 8, J - 16), :] = body
            xo[pl.ds(base + J - 8, 8), :] = tail
        return head, body, tail

    head, body, tail = lax.fori_loop(
        0, I // U, sweep_forward,
        (jnp.zeros((8, Z), F32), jnp.zeros((J - 16, Z), F32), jnp.zeros((8, Z), F32)))

    def sweep_backward(c, state):
        for u in range(U):
            i = I - 1 - (c * U + u)
            state = at(xr, I + i, J) * state + at(xs, i, J) * at(xo, i, J)
            to[pl.ds(i, J, stride=I), :] = state
        return state

    x_first = lax.fori_loop(0, I // U, sweep_backward, jnp.zeros((J, Z), F32))
    pack(xos, 0, jnp.concatenate([head, body, tail], axis=0), xrow)
    pack(xos, 1, x_first, xrow)
    push(xos, xor_, True, 1)

    load_y.wait()

    def span_forward(c, gain):
        for u in range(2):
            j = c * 2 + u
            ratio = yr[pl.ds(j, I, stride=J), :]
            scale = complement(ratio)
            put(yr0, j, I, ratio)
            put(tg, j, I, scale * at(tg, j, I))
            put(tc, j, I, scale * at(tc, j, I))
            put(to, j, I, scale * at(to, j, I))
            gain = ratio * gain
            put(ysc, j, I, gain)
        return gain

    y_gain = lax.fori_loop(0, J // 2, span_forward, jnp.ones((I, Z), F32))

    def span_backward(c, carry):
        gain, cross = carry
        for u in range(2):
            j = J - 1 - (c * 2 + u)
            ratio = yr[pl.ds(I * J + j, I, stride=J), :]
            scale = complement(ratio)
            put(yr1, j, I, ratio)
            put(ys1, j, I, scale)
            gain = ratio * gain
            cross = ratio * cross + scale * at(ysc, j, I)
            put(ygb, j, I, gain)
            put(ycc, j, I, cross)
        return gain, cross

    y_back, y_cross = lax.fori_loop(
        0, J // 2, span_backward, (jnp.ones((I, Z), F32), jnp.zeros((I, Z), F32)))
    pack(ygs, 0, y_gain, yrow)
    pack(ygs, 1, y_back, yrow)
    pack(ygs, 2, y_cross, yrow)
    push(ygs, ygr, False, 3)

    def chain(gains, sums, gr, sr, answers, mine, me, n, rows):
        gr[me] = gains[me]
        sr[me] = sums[me]
        state = jnp.zeros((rows, Z), F32)
        partial = []
        for k in range(n):
            answers[k, 0] = state
            partial.append(sr[k, 1] + gr[k, 2] * state)
            state = sr[k, 0] + gr[k, 0] * state
        state = jnp.zeros((rows, Z), F32)
        for k in reversed(range(n)):
            answers[k, 1] = state
            state = partial[k] + gr[k, 1] * state
        mine[me] = answers[me]

    arrived(xgr, 0)
    arrived(xor_, 1)
    chain(xgs, xos, xgr, xor_, xas, xar, mx, nx, xrow)
    push(xas, xar, True, 2)
    arrived(xar, 2)

    def across(s, state):
        for t in range(xrow):
            j = s * xrow + t
            a = xar[s, 0, t:t + 1, :]
            b = xar[s, 1, t:t + 1, :]
            source = at(to, j, I) + at(tg, j, I) * b + at(tc, j, I) * a
            state = at(yr0, j, I) * state + source
            put(yfw, j, I, state)
        return state

    y_last = lax.fori_loop(0, nx, across, jnp.zeros((I, Z), F32))

    def back(c, state):
        for u in range(2):
            j = J - 1 - (c * 2 + u)
            state = at(yr1, j, I) * state + at(ys1, j, I) * at(yfw, j, I)
            put(ycb, j, I, state)
        return state

    y_first = lax.fori_loop(0, J // 2, back, jnp.zeros((I, Z), F32))
    pack(yos, 0, y_last, yrow)
    pack(yos, 1, y_first, yrow)
    push(yos, yor, False, 4)

    sign = jnp.where(lax.broadcasted_iota(jnp.int32, (I, Z), 1) == Z // 2, 1.0, 0.0) - jnp.where(
        lax.broadcasted_iota(jnp.int32, (I, Z), 1) == Z // 2 - 1, 1.0, 0.0)
    station = lax.broadcasted_iota(jnp.int32, (I, J), 1)

    def own_jump(j, jump):
        found = jnp.sum(sign * p[pl.ds(2 * J + j, I, stride=J), :], axis=1, keepdims=True)
        return jnp.where(station == j, found, jump)

    jump = lax.fori_loop(0, J, own_jump, jnp.zeros((I, J), F32))

    stream = mx * I + lax.broadcasted_iota(jnp.int32, (I, J), 0)
    owner = jnp.transpose(mode[...])
    begin = lead[...]
    length = chord[...]
    onwing = jnp.logical_and(stream >= begin, stream < begin + length)
    weight = jnp.where(onwing, 0.5 + 2.5 * stream.astype(F32) / (I * nx), 0.0) / jnp.sqrt(
        length.astype(F32))

    arrived(ygr, 3)
    arrived(yor, 4)
    chain(ygs, yos, ygr, yor, yas, yar, my, ny, yrow)
    push(yas, yar, False, 5)
    arrived(yar, 5)
    for s in range(ny):
        ya[s * yrow:(s + 1) * yrow, :] = yar[s, 0]
        yb[s * yrow:(s + 1) * yrow, :] = yar[s, 1]

    def finish(j, jump):
        value = at(ycb, j, I) + at(ygb, j, I) * yb[...] + at(ycc, j, I) * ya[...]
        out[pl.ds(j, I, stride=J), :] = value
        found = jnp.sum(sign * value, axis=1, keepdims=True)
        return jump + jnp.where(station == j, found, 0.0)

    jump = lax.fori_loop(0, J, finish, jump)
    scaled = weight * jump
    for m in range(MODES):
        ls[m:m + 1, 0:J] = jnp.sum(jnp.where(owner == m, scaled, 0.0), axis=0, keepdims=True)

    def push_loads(k, _):
        peer = lax.rem(mx + k, nx)
        pltpu.make_async_remote_copy(
            src_ref=ls, dst_ref=lr.at[mx], send_sem=push_send.at[6], recv_sem=push_recv.at[6],
            device_id=(peer, my), device_id_type=MESH).start()
        return 0

    ls[:, J:] = jnp.zeros((MODES, Z - J), F32)
    lax.fori_loop(1, nx, push_loads, 0)
    lr[mx] = ls[...]
    arrived(lr, 6)
    total = lr[0]
    for k in range(1, nx):
        total = total + lr[k]
    loads[...] = total[:, 0:J]

    for halo in halos:
        halo.wait_send()
    for src, slot in ((xgs, 0), (xos, 1), (xas, 2), (ygs, 3), (yos, 4), (yas, 5), (lr, 6)):
        drained(src, slot)


def shards(nx, ny, potential, coefficient, shock_switch, x_factors, y_factors, wing_lead, wing_chord,
           panel_mode):
    I, J, Z = potential.shape
    cells = I * J
    xrow, yrow = J // nx, I // ny
    any_space = pl.BlockSpec(memory_space=pl.ANY)
    vmem = pl.BlockSpec(memory_space=pltpu.VMEM)
    block = pltpu.VMEM((cells, Z), F32)
    face = pltpu.VMEM((I, Z), F32)
    scratch = [
        pltpu.VMEM((cells + 3 * J, Z), F32),
        block,
        pltpu.VMEM((cells, Z), jnp.int32),
        pltpu.VMEM((2 * cells, Z), F32),
        pltpu.VMEM((2 * cells, Z), F32),
    ] + [block] * 15 + [face] * 4 + [
        pltpu.VMEM((2 * J, Z), F32),
        pltpu.VMEM((J, Z), F32),
        face,
    ]
    for n, rows in ((nx, xrow), (ny, yrow)):
        for members in (3, 2, 2):
            scratch += [pltpu.VMEM((n, members, rows, Z), F32)] * 2
    scratch += [
        pltpu.VMEM((MODES, Z), F32),
        pltpu.VMEM((nx, MODES, Z), F32),
        face,
        face,
        pltpu.SemaphoreType.DMA((5,)),
        pltpu.SemaphoreType.DMA((4,)),
        pltpu.SemaphoreType.DMA((4,)),
        pltpu.SemaphoreType.DMA((7,)),
        pltpu.SemaphoreType.DMA((7,)),
    ]
    correction, loads = pl.pallas_call(
        functools.partial(kernel, nx, ny, I, J, Z),
        out_shape=(
            jax.ShapeDtypeStruct((cells, Z), F32),
            jax.ShapeDtypeStruct((MODES, J), F32),
        ),
        in_specs=[any_space] * 5 + [vmem] * 3,
        out_specs=(vmem, vmem),
        scratch_shapes=scratch,
        compiler_params=pltpu.CompilerParams(
            collective_id=0, has_side_effects=True, vmem_limit_bytes=60 * 1024 * 1024),
        name="factored_step",
    )(
        potential.reshape(cells, Z),
        coefficient.reshape(cells, Z),
        shock_switch.reshape(cells, Z),
        x_factors.reshape(2 * cells, Z),
        y_factors.reshape(2 * cells, Z),
        wing_lead.reshape(1, J),
        wing_chord.reshape(1, J),
        panel_mode.T,
    )
    return correction.reshape(I, J, Z), loads


def solution(mesh):
    placed = (
        P("gx", "gy", None),
        P("gx", "gy", None),
        P("gx", "gy", None),
        P(None, "gx", "gy", None),
        P(None, "gx", "gy", None),
        P("gy"),
        P("gy"),
        P("gx", "gy"),
    )
    return jax.shard_map(
        functools.partial(shards, mesh.shape["gx"], mesh.shape["gy"]),
        mesh=mesh,
        in_specs=placed,
        out_specs=(P("gx", "gy", None), P(None, "gy")),
        check_vma=False,
    )
```

```python
import functools

import jax
import jax.numpy as jnp
from jax import lax
from jax.experimental import pallas as pl
from jax.experimental.pallas import tpu as pltpu
from jax.sharding import PartitionSpec as P

MODES = 2
MESH = pl.DeviceIdType.MESH
F32 = jnp.float32


def complement(ratio):
    return jnp.sqrt(1.0 - ratio * ratio)


def kernel(nx, ny, I, J, Z, *refs):
    (pot, coef, switch, xf, yf, lead, chord, mode, out, loads,
     p, cf, sw, xr, yr, xq, xs, xg, xo,
     to, tg, tc, yr0, ysc, yr1, ys1, yfw, ycb, ygb, ycc,
     face_hi, face_lo, halo_lo, halo_hi, halo_prev, halo_next, strip,
     xgs, xgr, xos, xor_, xas, xar, ygs, ygr, yos, yor, yas, yar, ls, lr, ya, yb,
     mgs, mgr, mos, mor, wide,
     load_sem, halo_send, halo_recv, push_send, push_recv) = refs
    mx = lax.axis_index("gx")
    my = lax.axis_index("gy")
    xrow, yrow = J // nx, I // ny
    U = 8

    barrier = pltpu.get_barrier_semaphore()

    def greet_x(k, _):
        pl.semaphore_signal(barrier, inc=1, device_id=(lax.rem(mx + k, nx), my), device_id_type=MESH)
        return 0

    def greet_y(k, _):
        pl.semaphore_signal(barrier, inc=1, device_id=(mx, lax.rem(my + k, ny)), device_id_type=MESH)
        return 0

    lax.fori_loop(1, nx, greet_x, 0)
    lax.fori_loop(1, ny, greet_y, 0)

    load_p = pltpu.make_async_copy(pot, p.at[pl.ds(2 * J, I * J), :], load_sem.at[0])
    load_x = pltpu.make_async_copy(xf, xr, load_sem.at[1])
    load_c = pltpu.make_async_copy(coef, cf, load_sem.at[2])
    load_s = pltpu.make_async_copy(switch, sw, load_sem.at[3])
    load_y = pltpu.make_async_copy(yf, yr, load_sem.at[4])
    for load in (load_p, load_x, load_c, load_s, load_y):
        load.start()

    def push(src, dst, along_x, slot, same=False):
        me, n = (mx, nx) if along_x else (my, ny)

        def body(k, _):
            peer = lax.rem(me + k, n)
            pltpu.make_async_remote_copy(
                src_ref=src if same else src.at[peer],
                dst_ref=dst.at[me],
                send_sem=push_send.at[slot],
                recv_sem=push_recv.at[slot],
                device_id=(peer, my) if along_x else (mx, peer),
                device_id_type=MESH,
            ).start()
            return 0

        lax.fori_loop(1, n, body, 0)

    def arrived(dst, slot):
        part = dst.at[pl.ds(0, dst.shape[0] - 1)]
        pltpu.make_async_copy(part, part, push_recv.at[slot]).wait()

    def drained(src, slot):
        part = src.at[pl.ds(0, src.shape[0] - 1)]
        pltpu.make_async_copy(part, part, push_send.at[slot]).wait()

    def at(ref, index, rows):
        return ref[pl.ds(pl.multiple_of(index * rows, 8), rows), :]

    def put(ref, index, rows, value):
        ref[pl.ds(pl.multiple_of(index * rows, 8), rows), :] = value

    def pack(dst, member, value, rows):
        total = value.shape[0]
        strip[0:total, :] = value
        for s in range(total // rows):
            dst[s, member] = strip[s * rows:(s + 1) * rows, :]

    row = lax.broadcasted_iota(jnp.int32, (J, Z), 0)
    lane = lax.broadcasted_iota(jnp.int32, (J, Z), 1)
    row8 = lax.broadcasted_iota(jnp.int32, (8, Z), 0)

    zero_line = jnp.zeros((J, Z), F32)
    p[0:J, :] = zero_line
    p[J:2 * J, :] = zero_line
    p[(I + 2) * J:(I + 3) * J, :] = zero_line
    load_p.wait()
    face_hi[...] = p[pl.ds(2 * J + J - 1, I, stride=J), :]
    face_lo[...] = p[pl.ds(2 * J, I, stride=J), :]

    pl.semaphore_wait(barrier, nx + ny - 2)

    def neighbour(src, dst, slot, device):
        return pltpu.make_async_remote_copy(
            src_ref=src, dst_ref=dst, send_sem=halo_send.at[slot], recv_sem=halo_recv.at[slot],
            device_id=device, device_id_type=MESH)

    left, right = lax.rem(mx + nx - 1, nx), lax.rem(mx + 1, nx)
    down, up = lax.rem(my + ny - 1, ny), lax.rem(my + 1, ny)
    halos = (
        neighbour(pot.at[pl.ds((I - 2) * J, 2 * J), :], halo_prev, 0, (right, my)),
        neighbour(pot.at[pl.ds(0, J), :], halo_next, 1, (left, my)),
        neighbour(face_hi, halo_lo, 2, (mx, up)),
        neighbour(face_lo, halo_hi, 3, (mx, down)),
    )
    for halo in halos:
        halo.start()

    pair = lax.broadcasted_iota(jnp.int32, (I, Z), 1) // 2

    def pick(value, j, kept):
        return jnp.where(pair == j, pltpu.roll(value, lax.rem(2 * j + Z // 2 + 1, Z), 1), kept)

    def planes(upper, lower):
        turned = jnp.transpose(jnp.concatenate([upper, lower], axis=0))
        return turned[Z // 2 - 1:Z // 2 + 1]

    load_x.wait()

    def gain_forward(c, gain):
        for u in range(U):
            i = c * U + u
            ratio = at(xr, i, J)
            put(xq, i, J, 0.25 * complement(ratio))
            gain = ratio * gain
            put(xg, i, J, gain)
        return gain

    x_gain = lax.fori_loop(0, I // U, gain_forward, jnp.ones((J, Z), F32))

    def gain_backward(c, carry):
        gain, cross = carry
        for u in range(U):
            i = I - 1 - (c * U + u)
            ratio = at(xr, I + i, J)
            scale = complement(ratio)
            put(xs, i, J, scale)
            gain = ratio * gain
            cross = ratio * cross + scale * at(xg, i, J)
            tg[pl.ds(i, J, stride=I), :] = gain
            tc[pl.ds(i, J, stride=I), :] = cross
        return gain, cross

    x_back, x_cross = lax.fori_loop(
        0, I // U, gain_backward, (jnp.ones((J, Z), F32), jnp.zeros((J, Z), F32)))
    pack(xgs, 0, x_gain, xrow)
    pack(xgs, 1, x_back, xrow)
    pack(xgs, 2, x_cross, xrow)

    push(xgs, xgr, True, 0)

    load_c.wait()
    load_s.wait()

    def forcing(c, _):
        for u in range(2):
            i = c * 2 + u
            before2, before, center, after = (at(p, i + d, J) for d in range(4))
            second = jnp.where(at(sw, i, J) == 1, center - 2.0 * before + before2,
                               after - 2.0 * center + before)
            span = jnp.where(row == 0, 0.0, pltpu.roll(center, 1, 0)) + jnp.where(
                row == J - 1, 0.0, pltpu.roll(center, J - 1, 0))
            normal = jnp.where(lane == 0, 0.0, pltpu.roll(center, 1, 1)) + jnp.where(
                lane == Z - 1, 0.0, pltpu.roll(center, Z - 1, 1))
            residual = at(cf, i, J) * second + (span - 2.0 * center) + (normal - 2.0 * center)
            put(xo, i, J, at(xq, i, J) * residual)
        return 0

    lax.fori_loop(0, I // 2, forcing, 0)

    for halo in halos:
        halo.wait_recv()

    before = jnp.where(mx == 0, 0.0, halo_prev[J:2 * J, :])
    before2 = jnp.where(mx == 0, 0.0, halo_prev[0:J, :])
    after = jnp.where(mx == nx - 1, 0.0, halo_next[...])
    first = jnp.where(at(sw, 0, J) == 1, before2 - 2.0 * before, before)
    second = jnp.where(at(sw, 1, J) == 1, before, 0.0)
    last = jnp.where(at(sw, I - 1, J) == 1, 0.0, after)
    for i, term in ((0, first), (1, second), (I - 1, last)):
        put(xo, i, J, at(xo, i, J) + at(xq, i, J) * (at(cf, i, J) * term))
    low = jnp.logical_and(row8 == 0, my > 0)
    high = jnp.logical_and(row8 == 7, my < ny - 1)

    def sweep_forward(c, carry):
        head, body, tail = carry
        low8 = at(halo_lo, c, U)
        high8 = at(halo_hi, c, U)
        for u in range(U):
            base = pl.multiple_of((c * U + u) * J, 8)
            r = xr[pl.ds(base, J), :]
            f = xo[pl.ds(base, J), :]
            q0 = xq[pl.ds(base, 8), :]
            q3 = xq[pl.ds(base + J - 8, 8), :]
            head = r[0:8] * head + (f[0:8] + q0 * jnp.where(low, low8[u:u + 1], 0.0))
            body = r[8:J - 8] * body + f[8:J - 8]
            tail = r[J - 8:] * tail + (f[J - 8:] + q3 * jnp.where(high, high8[u:u + 1], 0.0))
            xo[pl.ds(base, 8), :] = head
            xo[pl.ds(base + 8, J - 16), :] = body
            xo[pl.ds(base + J - 8, 8), :] = tail
        return head, body, tail

    head, body, tail = lax.fori_loop(
        0, I // U, sweep_forward,
        (jnp.zeros((8, Z), F32), jnp.zeros((J - 16, Z), F32), jnp.zeros((8, Z), F32)))

    def sweep_backward(c, state):
        for u in range(U):
            i = I - 1 - (c * U + u)
            state = at(xr, I + i, J) * state + at(xs, i, J) * at(xo, i, J)
            to[pl.ds(i, J, stride=I), :] = state
        return state

    x_first = lax.fori_loop(0, I // U, sweep_backward, jnp.zeros((J, Z), F32))
    pack(xos, 0, jnp.concatenate([head, body, tail], axis=0), xrow)
    pack(xos, 1, x_first, xrow)
    push(xos, xor_, True, 1)

    load_y.wait()

    def span_forward(c, gain):
        for u in range(2):
            j = c * 2 + u
            ratio = yr[pl.ds(j, I, stride=J), :]
            scale = complement(ratio)
            put(yr0, j, I, ratio)
            put(tg, j, I, scale * at(tg, j, I))
            put(tc, j, I, scale * at(tc, j, I))
            put(to, j, I, scale * at(to, j, I))
            gain = ratio * gain
            put(ysc, j, I, gain)
        return gain

    y_gain = lax.fori_loop(0, J // 2, span_forward, jnp.ones((I, Z), F32))

    def span_backward(c, carry):
        gain, cross, gains2, crosses2 = carry
        for u in range(2):
            j = J - 1 - (c * 2 + u)
            ratio = yr[pl.ds(I * J + j, I, stride=J), :]
            scale = complement(ratio)
            put(yr1, j, I, ratio)
            put(ys1, j, I, scale)
            gain = ratio * gain
            cross = ratio * cross + scale * at(ysc, j, I)
            put(ygb, j, I, gain)
            put(ycc, j, I, cross)
            gains2 = pick(gain, j, gains2)
            crosses2 = pick(cross, j, crosses2)
        return gain, cross, gains2, crosses2

    zero_face = jnp.zeros((I, Z), F32)
    y_back, y_cross, gains2, crosses2 = lax.fori_loop(
        0, J // 2, span_backward, (jnp.ones((I, Z), F32), zero_face, zero_face, zero_face))
    wide[0:I, :] = gains2
    wide[I:2 * I, :] = crosses2
    pack(ygs, 0, y_gain, yrow)
    pack(ygs, 1, y_back, yrow)
    pack(ygs, 2, y_cross, yrow)
    push(ygs, ygr, False, 3)
    mgs[0] = planes(y_gain, y_back)
    mgs[1] = planes(y_cross, y_cross)
    push(mgs, mgr, False, 7, True)

    def chain(gains, sums, gr, sr, answers, mine, me, n, rows):
        gr[me] = gains[me]
        sr[me] = sums[me]
        state = jnp.zeros((rows, Z), F32)
        partial = []
        for k in range(n):
            answers[k, 0] = state
            partial.append(sr[k, 1] + gr[k, 2] * state)
            state = sr[k, 0] + gr[k, 0] * state
        state = jnp.zeros((rows, Z), F32)
        for k in reversed(range(n)):
            answers[k, 1] = state
            state = partial[k] + gr[k, 1] * state
        mine[me] = answers[me]

    arrived(xgr, 0)
    arrived(xor_, 1)
    chain(xgs, xos, xgr, xor_, xas, xar, mx, nx, xrow)
    push(xas, xar, True, 2)
    arrived(xar, 2)

    def across(s, state):
        for t in range(xrow):
            j = s * xrow + t
            a = xar[s, 0, t:t + 1, :]
            b = xar[s, 1, t:t + 1, :]
            source = at(to, j, I) + at(tg, j, I) * b + at(tc, j, I) * a
            state = at(yr0, j, I) * state + source
            put(yfw, j, I, state)
        return state

    y_last = lax.fori_loop(0, nx, across, jnp.zeros((I, Z), F32))

    def back(c, state):
        for u in range(2):
            j = J - 1 - (c * 2 + u)
            state = at(yr1, j, I) * state + at(ys1, j, I) * at(yfw, j, I)
            put(ycb, j, I, state)
        return state

    y_first = lax.fori_loop(0, J // 2, back, jnp.zeros((I, Z), F32))
    pack(yos, 0, y_last, yrow)
    pack(yos, 1, y_first, yrow)
    push(yos, yor, False, 4)

    mos[...] = planes(y_last, y_first)
    push(mos, mor, False, 8, True)

    def own_planes(j, kept):
        return pick(p[pl.ds(2 * J + j, I, stride=J), :] + at(ycb, j, I), j, kept)

    jump = lax.fori_loop(0, J, own_planes, zero_face)

    stream = mx * I + lax.broadcasted_iota(jnp.int32, (J, I), 1)
    begin = jnp.transpose(jnp.broadcast_to(lead[...], (8, J)))[:, 0:1]
    length = jnp.transpose(jnp.broadcast_to(chord[...], (8, J)))[:, 0:1]
    onwing = jnp.logical_and(stream >= begin, stream < begin + length)
    weight = jnp.where(onwing, 0.5 + 2.5 * stream.astype(F32) / (I * nx), 0.0) / jnp.sqrt(
        length.astype(F32))
    weights = []
    for m in range(MODES):
        own = jnp.concatenate(
            [jnp.where(mode[...] == m, weight, 0.0), jnp.zeros((J, Z - I), F32)], axis=1)
        rows = 2 * I + m * 2 * J
        wide[pl.ds(rows, J, stride=2), :] = -own
        wide[pl.ds(rows + 1, J, stride=2), :] = own
        weights.append(jnp.transpose(wide[rows:rows + 2 * J, :])[0:I])

    arrived(ygr, 3)
    arrived(yor, 4)
    chain(ygs, yos, ygr, yor, yas, yar, my, ny, yrow)
    push(yas, yar, False, 5)

    arrived(mgr, 7)
    arrived(mor, 8)
    mgr[my] = mgs[...]
    mor[my] = mos[...]
    state = jnp.zeros((2, Z), F32)
    from_left = from_right = state
    partial = []
    for k in range(ny):
        from_left = jnp.where(my == k, state, from_left)
        partial.append(mor[k] + mgr[k, 1] * pltpu.roll(state, I, 1))
        state = mor[k] + mgr[k, 0] * state
    state = jnp.zeros((2, Z), F32)
    for k in reversed(range(ny)):
        from_right = jnp.where(my == k, state, from_right)
        state = partial[k] + mgr[k, 0] * state
    lanes = lax.broadcasted_iota(jnp.int32, (2, Z), 1)
    states = jnp.concatenate(
        [jnp.where(lanes < I, from_left, from_right), jnp.zeros((6, Z), F32)], axis=0)
    states = jnp.transpose(states)
    odd = lax.rem(lax.broadcasted_iota(jnp.int32, (I, Z), 1), 2) == 1
    left_state = jnp.where(odd, states[0:I, 1:2], states[0:I, 0:1])
    right_state = jnp.where(odd, states[I:2 * I, 1:2], states[I:2 * I, 0:1])
    jump = jump + wide[0:I, :] * right_state + wide[I:2 * I, :] * left_state
    for m in range(MODES):
        ls[m:m + 1, 0:2 * J] = jnp.sum(weights[m] * jump[:, 0:2 * J], axis=0, keepdims=True)

    def push_loads(k, _):
        peer = lax.rem(mx + k, nx)
        pltpu.make_async_remote_copy(
            src_ref=ls, dst_ref=lr.at[mx], send_sem=push_send.at[6], recv_sem=push_recv.at[6],
            device_id=(peer, my), device_id_type=MESH).start()
        return 0

    ls[:, 2 * J:] = jnp.zeros((MODES, Z - 2 * J), F32)
    lax.fori_loop(1, nx, push_loads, 0)
    lr[mx] = ls[...]

    arrived(yar, 5)
    for s in range(ny):
        ya[s * yrow:(s + 1) * yrow, :] = yar[s, 0]
        yb[s * yrow:(s + 1) * yrow, :] = yar[s, 1]
    a = ya[...]
    b = yb[...]

    def finish(j, _):
        out[pl.ds(j, I, stride=J), :] = at(ycb, j, I) + at(ygb, j, I) * b + at(ycc, j, I) * a
        return 0

    lax.fori_loop(0, J, finish, 0)

    arrived(lr, 6)
    total = lr[0]
    for k in range(1, nx):
        total = total + lr[k]
    fold = lax.broadcasted_iota(jnp.int32, (Z, J), 0) // 2 == lax.broadcasted_iota(
        jnp.int32, (Z, J), 1)
    loads[...] = jnp.dot(total, fold.astype(F32), precision=lax.Precision.HIGHEST,
                         preferred_element_type=F32)

    for halo in halos:
        halo.wait_send()
    for src, slot in ((xgs, 0), (xos, 1), (xas, 2), (ygs, 3), (yos, 4), (yas, 5), (lr, 6), (mgr, 7),
                      (mor, 8)):
        drained(src, slot)


def shards(nx, ny, potential, coefficient, shock_switch, x_factors, y_factors, wing_lead, wing_chord,
           panel_mode):
    I, J, Z = potential.shape
    cells = I * J
    xrow, yrow = J // nx, I // ny
    any_space = pl.BlockSpec(memory_space=pl.ANY)
    vmem = pl.BlockSpec(memory_space=pltpu.VMEM)
    block = pltpu.VMEM((cells, Z), F32)
    face = pltpu.VMEM((I, Z), F32)
    scratch = [
        pltpu.VMEM((cells + 3 * J, Z), F32),
        block,
        pltpu.VMEM((cells, Z), jnp.int32),
        pltpu.VMEM((2 * cells, Z), F32),
        pltpu.VMEM((2 * cells, Z), F32),
    ] + [block] * 15 + [face] * 4 + [
        pltpu.VMEM((2 * J, Z), F32),
        pltpu.VMEM((J, Z), F32),
        face,
    ]
    for n, rows in ((nx, xrow), (ny, yrow)):
        for members in (3, 2, 2):
            scratch += [pltpu.VMEM((n, members, rows, Z), F32)] * 2
    scratch += [
        pltpu.VMEM((MODES, Z), F32),
        pltpu.VMEM((nx, MODES, Z), F32),
        face,
        face,
        pltpu.VMEM((2, 2, Z), F32),
        pltpu.VMEM((ny, 2, 2, Z), F32),
        pltpu.VMEM((2, Z), F32),
        pltpu.VMEM((ny, 2, Z), F32),
        pltpu.VMEM((2 * I + 2 * J * MODES, Z), F32),
        pltpu.SemaphoreType.DMA((5,)),
        pltpu.SemaphoreType.DMA((4,)),
        pltpu.SemaphoreType.DMA((4,)),
        pltpu.SemaphoreType.DMA((9,)),
        pltpu.SemaphoreType.DMA((9,)),
    ]
    correction, loads = pl.pallas_call(
        functools.partial(kernel, nx, ny, I, J, Z),
        out_shape=(
            pltpu.VMEM((cells, Z), F32),
            pltpu.VMEM((MODES, J), F32),
        ),
        in_specs=[any_space] * 5 + [vmem] * 3,
        out_specs=(vmem, vmem),
        scratch_shapes=scratch,
        compiler_params=pltpu.CompilerParams(
            collective_id=0, has_side_effects=True, vmem_limit_bytes=60 * 1024 * 1024),
        name="factored_step",
    )(
        potential.reshape(cells, Z),
        coefficient.reshape(cells, Z),
        shock_switch.reshape(cells, Z),
        x_factors.reshape(2 * cells, Z),
        y_factors.reshape(2 * cells, Z),
        wing_lead.reshape(1, J),
        wing_chord.reshape(1, J),
        panel_mode.T,
    )
    return correction.reshape(I, J, Z), loads


def solution(mesh):
    placed = (
        P("gx", "gy", None),
        P("gx", "gy", None),
        P("gx", "gy", None),
        P(None, "gx", "gy", None),
        P(None, "gx", "gy", None),
        P("gy"),
        P("gy"),
        P("gx", "gy"),
    )
    return jax.shard_map(
        functools.partial(shards, mesh.shape["gx"], mesh.shape["gy"]),
        mesh=mesh,
        in_specs=placed,
        out_specs=(P("gx", "gy", None), P(None, "gy")),
        check_vma=False,
    )
```

```python
import functools

import jax
import jax.numpy as jnp
from jax import lax
from jax.experimental import pallas as pl
from jax.experimental.pallas import tpu as pltpu
from jax.sharding import PartitionSpec as P

MODES = 2
MESH = pl.DeviceIdType.MESH
F32 = jnp.float32


def complement(ratio):
    return jnp.sqrt(1.0 - ratio * ratio)


def kernel(nx, ny, I, J, Z, *refs):
    (pot, coef, switch, xf, yf, lead_hbm, chord_hbm, mode_hbm, ycb, ygb, ycc, yar, loads,
     p, cf, sw, xr, yr, xq, xs, xg, xo,
     to, tg, tc, yr0, ysc, yr1, ys1, yfw,
     face_hi, face_lo, halo_lo, halo_hi, halo_prev, halo_next, strip,
     xgs, xgr, xos, xor_, xas, xar, ygs, ygr, yos, yor, yas, ls, lr,
     mgs, mgr, mos, mor, wide, lead, chord, mode,
     load_sem, halo_send, halo_recv, push_send, push_recv) = refs
    mx = lax.axis_index("gx")
    my = lax.axis_index("gy")
    xrow, yrow = J // nx, I // ny
    U = 8

    barrier = pltpu.get_barrier_semaphore()

    def greet_x(k, _):
        pl.semaphore_signal(barrier, inc=1, device_id=(lax.rem(mx + k, nx), my), device_id_type=MESH)
        return 0

    def greet_y(k, _):
        pl.semaphore_signal(barrier, inc=1, device_id=(mx, lax.rem(my + k, ny)), device_id_type=MESH)
        return 0

    lax.fori_loop(1, nx, greet_x, 0)
    lax.fori_loop(1, ny, greet_y, 0)

    load_p = pltpu.make_async_copy(pot, p.at[pl.ds(2 * J, I * J), :], load_sem.at[0])
    load_x = pltpu.make_async_copy(xf, xr, load_sem.at[1])
    load_c = pltpu.make_async_copy(coef, cf, load_sem.at[2])
    load_s = pltpu.make_async_copy(switch, sw, load_sem.at[3])
    load_y = pltpu.make_async_copy(yf, yr, load_sem.at[4])
    load_w = [pltpu.make_async_copy(src, dst, load_sem.at[slot]) for src, dst, slot in (
        (lead_hbm, lead, 5), (chord_hbm, chord, 6), (mode_hbm, mode, 7))]
    for load in [load_p, load_x, load_c, load_s, load_y] + load_w:
        load.start()

    def push(src, dst, along_x, slot, same=False):
        me, n = (mx, nx) if along_x else (my, ny)

        def body(k, _):
            peer = lax.rem(me + k, n)
            pltpu.make_async_remote_copy(
                src_ref=src if same else src.at[peer],
                dst_ref=dst.at[me],
                send_sem=push_send.at[slot],
                recv_sem=push_recv.at[slot],
                device_id=(peer, my) if along_x else (mx, peer),
                device_id_type=MESH,
            ).start()
            return 0

        lax.fori_loop(1, n, body, 0)

    def arrived(dst, slot):
        part = dst.at[pl.ds(0, dst.shape[0] - 1)]
        pltpu.make_async_copy(part, part, push_recv.at[slot]).wait()

    def drained(src, slot):
        part = src.at[pl.ds(0, src.shape[0] - 1)]
        pltpu.make_async_copy(part, part, push_send.at[slot]).wait()

    def at(ref, index, rows):
        return ref[pl.ds(pl.multiple_of(index * rows, 8), rows), :]

    def put(ref, index, rows, value):
        ref[pl.ds(pl.multiple_of(index * rows, 8), rows), :] = value

    def pack(dst, member, value, rows):
        total = value.shape[0]
        strip[0:total, :] = value
        for s in range(total // rows):
            dst[s, member] = strip[s * rows:(s + 1) * rows, :]

    row = lax.broadcasted_iota(jnp.int32, (J, Z), 0)
    lane = lax.broadcasted_iota(jnp.int32, (J, Z), 1)
    row8 = lax.broadcasted_iota(jnp.int32, (8, Z), 0)

    zero_line = jnp.zeros((J, Z), F32)
    p[0:J, :] = zero_line
    p[J:2 * J, :] = zero_line
    p[(I + 2) * J:(I + 3) * J, :] = zero_line
    load_p.wait()
    face_hi[...] = p[pl.ds(2 * J + J - 1, I, stride=J), :]
    face_lo[...] = p[pl.ds(2 * J, I, stride=J), :]

    pl.semaphore_wait(barrier, nx + ny - 2)

    def neighbour(src, dst, slot, device):
        return pltpu.make_async_remote_copy(
            src_ref=src, dst_ref=dst, send_sem=halo_send.at[slot], recv_sem=halo_recv.at[slot],
            device_id=device, device_id_type=MESH)

    left, right = lax.rem(mx + nx - 1, nx), lax.rem(mx + 1, nx)
    down, up = lax.rem(my + ny - 1, ny), lax.rem(my + 1, ny)
    halos = (
        neighbour(pot.at[pl.ds((I - 2) * J, 2 * J), :], halo_prev, 0, (right, my)),
        neighbour(pot.at[pl.ds(0, J), :], halo_next, 1, (left, my)),
        neighbour(face_hi, halo_lo, 2, (mx, up)),
        neighbour(face_lo, halo_hi, 3, (mx, down)),
    )
    for halo in halos:
        halo.start()

    pair = lax.broadcasted_iota(jnp.int32, (I, Z), 1) // 2

    def pick(value, j, kept):
        return jnp.where(pair == j, pltpu.roll(value, lax.rem(2 * j + Z // 2 + 1, Z), 1), kept)

    def planes(upper, lower):
        turned = jnp.transpose(jnp.concatenate([upper, lower], axis=0))
        return turned[Z // 2 - 1:Z // 2 + 1]

    load_x.wait()

    def gain_forward(c, gain):
        for u in range(U):
            i = c * U + u
            ratio = at(xr, i, J)
            put(xq, i, J, 0.25 * complement(ratio))
            gain = ratio * gain
            put(xg, i, J, gain)
        return gain

    x_gain = lax.fori_loop(0, I // U, gain_forward, jnp.ones((J, Z), F32))

    def gain_backward(c, carry):
        gain, cross = carry
        for u in range(U):
            i = I - 1 - (c * U + u)
            ratio = at(xr, I + i, J)
            scale = complement(ratio)
            put(xs, i, J, scale)
            gain = ratio * gain
            cross = ratio * cross + scale * at(xg, i, J)
            tg[pl.ds(i, J, stride=I), :] = gain
            tc[pl.ds(i, J, stride=I), :] = cross
        return gain, cross

    x_back, x_cross = lax.fori_loop(
        0, I // U, gain_backward, (jnp.ones((J, Z), F32), jnp.zeros((J, Z), F32)))
    pack(xgs, 0, x_gain, xrow)
    pack(xgs, 1, x_back, xrow)
    pack(xgs, 2, x_cross, xrow)

    push(xgs, xgr, True, 0)

    load_c.wait()
    load_s.wait()

    def forcing(c, _):
        for u in range(2):
            i = c * 2 + u
            before2, before, center, after = (at(p, i + d, J) for d in range(4))
            second = jnp.where(at(sw, i, J) == 1, center - 2.0 * before + before2,
                               after - 2.0 * center + before)
            span = jnp.where(row == 0, 0.0, pltpu.roll(center, 1, 0)) + jnp.where(
                row == J - 1, 0.0, pltpu.roll(center, J - 1, 0))
            normal = jnp.where(lane == 0, 0.0, pltpu.roll(center, 1, 1)) + jnp.where(
                lane == Z - 1, 0.0, pltpu.roll(center, Z - 1, 1))
            residual = at(cf, i, J) * second + (span - 2.0 * center) + (normal - 2.0 * center)
            put(xo, i, J, at(xq, i, J) * residual)
        return 0

    lax.fori_loop(0, I // 2, forcing, 0)

    for halo in halos:
        halo.wait_recv()

    before = jnp.where(mx == 0, 0.0, halo_prev[J:2 * J, :])
    before2 = jnp.where(mx == 0, 0.0, halo_prev[0:J, :])
    after = jnp.where(mx == nx - 1, 0.0, halo_next[...])
    first = jnp.where(at(sw, 0, J) == 1, before2 - 2.0 * before, before)
    second = jnp.where(at(sw, 1, J) == 1, before, 0.0)
    last = jnp.where(at(sw, I - 1, J) == 1, 0.0, after)
    for i, term in ((0, first), (1, second), (I - 1, last)):
        put(xo, i, J, at(xo, i, J) + at(xq, i, J) * (at(cf, i, J) * term))
    low = jnp.logical_and(row8 == 0, my > 0)
    high = jnp.logical_and(row8 == 7, my < ny - 1)

    def sweep_forward(c, carry):
        head, body, tail = carry
        low8 = at(halo_lo, c, U)
        high8 = at(halo_hi, c, U)
        for u in range(U):
            base = pl.multiple_of((c * U + u) * J, 8)
            r = xr[pl.ds(base, J), :]
            f = xo[pl.ds(base, J), :]
            q0 = xq[pl.ds(base, 8), :]
            q3 = xq[pl.ds(base + J - 8, 8), :]
            head = r[0:8] * head + (f[0:8] + q0 * jnp.where(low, low8[u:u + 1], 0.0))
            body = r[8:J - 8] * body + f[8:J - 8]
            tail = r[J - 8:] * tail + (f[J - 8:] + q3 * jnp.where(high, high8[u:u + 1], 0.0))
            xo[pl.ds(base, 8), :] = head
            xo[pl.ds(base + 8, J - 16), :] = body
            xo[pl.ds(base + J - 8, 8), :] = tail
        return head, body, tail

    head, body, tail = lax.fori_loop(
        0, I // U, sweep_forward,
        (jnp.zeros((8, Z), F32), jnp.zeros((J - 16, Z), F32), jnp.zeros((8, Z), F32)))

    def sweep_backward(c, state):
        for u in range(U):
            i = I - 1 - (c * U + u)
            state = at(xr, I + i, J) * state + at(xs, i, J) * at(xo, i, J)
            to[pl.ds(i, J, stride=I), :] = state
        return state

    x_first = lax.fori_loop(0, I // U, sweep_backward, jnp.zeros((J, Z), F32))
    pack(xos, 0, jnp.concatenate([head, body, tail], axis=0), xrow)
    pack(xos, 1, x_first, xrow)
    push(xos, xor_, True, 1)

    load_y.wait()

    def span_forward(c, gain):
        for u in range(2):
            j = c * 2 + u
            ratio = yr[pl.ds(j, I, stride=J), :]
            scale = complement(ratio)
            put(yr0, j, I, ratio)
            put(tg, j, I, scale * at(tg, j, I))
            put(tc, j, I, scale * at(tc, j, I))
            put(to, j, I, scale * at(to, j, I))
            gain = ratio * gain
            put(ysc, j, I, gain)
        return gain

    y_gain = lax.fori_loop(0, J // 2, span_forward, jnp.ones((I, Z), F32))

    def chain(gains, sums, gr, sr, answers, mine, me, n, rows):
        gr[me] = gains[me]
        sr[me] = sums[me]
        state = jnp.zeros((rows, Z), F32)
        partial = []
        for k in range(n):
            answers[k, 0] = state
            partial.append(sr[k, 1] + gr[k, 2] * state)
            state = sr[k, 0] + gr[k, 0] * state
        state = jnp.zeros((rows, Z), F32)
        for k in reversed(range(n)):
            answers[k, 1] = state
            state = partial[k] + gr[k, 1] * state
        mine[me] = answers[me]

    arrived(xgr, 0)
    arrived(xor_, 1)
    chain(xgs, xos, xgr, xor_, xas, xar, mx, nx, xrow)
    push(xas, xar, True, 2)

    def span_backward(c, carry):
        gain, cross, gains2, crosses2 = carry
        for u in range(2):
            j = J - 1 - (c * 2 + u)
            ratio = yr[pl.ds(I * J + j, I, stride=J), :]
            scale = complement(ratio)
            put(yr1, j, I, ratio)
            put(ys1, j, I, scale)
            gain = ratio * gain
            cross = ratio * cross + scale * at(ysc, j, I)
            put(ygb, j, I, gain)
            put(ycc, j, I, cross)
            gains2 = pick(gain, j, gains2)
            crosses2 = pick(cross, j, crosses2)
        return gain, cross, gains2, crosses2

    zero_face = jnp.zeros((I, Z), F32)
    y_back, y_cross, gains2, crosses2 = lax.fori_loop(
        0, J // 2, span_backward, (jnp.ones((I, Z), F32), zero_face, zero_face, zero_face))
    wide[0:I, :] = gains2
    wide[I:2 * I, :] = crosses2
    pack(ygs, 0, y_gain, yrow)
    pack(ygs, 1, y_back, yrow)
    pack(ygs, 2, y_cross, yrow)
    push(ygs, ygr, False, 3)
    mgs[0] = planes(y_gain, y_back)
    mgs[1] = planes(y_cross, y_cross)
    push(mgs, mgr, False, 7, True)

    arrived(xar, 2)

    def across(s, state):
        for t in range(xrow):
            j = s * xrow + t
            a = xar[s, 0, t:t + 1, :]
            b = xar[s, 1, t:t + 1, :]
            source = at(to, j, I) + at(tg, j, I) * b + at(tc, j, I) * a
            state = at(yr0, j, I) * state + source
            put(yfw, j, I, state)
        return state

    y_last = lax.fori_loop(0, nx, across, jnp.zeros((I, Z), F32))

    def back(c, state):
        for u in range(2):
            j = J - 1 - (c * 2 + u)
            state = at(yr1, j, I) * state + at(ys1, j, I) * at(yfw, j, I)
            put(ycb, j, I, state)
        return state

    y_first = lax.fori_loop(0, J // 2, back, jnp.zeros((I, Z), F32))
    pack(yos, 0, y_last, yrow)
    pack(yos, 1, y_first, yrow)
    push(yos, yor, False, 4)

    mos[...] = planes(y_last, y_first)
    push(mos, mor, False, 8, True)

    def own_planes(j, kept):
        return pick(p[pl.ds(2 * J + j, I, stride=J), :] + at(ycb, j, I), j, kept)

    jump = lax.fori_loop(0, J, own_planes, zero_face)

    for load in load_w:
        load.wait()
    stream = mx * I + lax.broadcasted_iota(jnp.int32, (J, I), 1)
    begin = jnp.transpose(jnp.broadcast_to(lead[...], (8, J)))[:, 0:1]
    length = jnp.transpose(jnp.broadcast_to(chord[...], (8, J)))[:, 0:1]
    onwing = jnp.logical_and(stream >= begin, stream < begin + length)
    weight = jnp.where(onwing, 0.5 + 2.5 * stream.astype(F32) / (I * nx), 0.0) / jnp.sqrt(
        length.astype(F32))
    weights = []
    for m in range(MODES):
        own = jnp.concatenate(
            [jnp.where(mode[...] == m, weight, 0.0), jnp.zeros((J, Z - I), F32)], axis=1)
        rows = 2 * I + m * 2 * J
        wide[pl.ds(rows, J, stride=2), :] = -own
        wide[pl.ds(rows + 1, J, stride=2), :] = own
        weights.append(jnp.transpose(wide[rows:rows + 2 * J, :])[0:I])

    arrived(ygr, 3)
    arrived(yor, 4)
    chain(ygs, yos, ygr, yor, yas, yar, my, ny, yrow)
    push(yas, yar, False, 5)

    arrived(mgr, 7)
    arrived(mor, 8)
    mgr[my] = mgs[...]
    mor[my] = mos[...]
    state = jnp.zeros((2, Z), F32)
    from_left = from_right = state
    partial = []
    for k in range(ny):
        from_left = jnp.where(my == k, state, from_left)
        partial.append(mor[k] + mgr[k, 1] * pltpu.roll(state, I, 1))
        state = mor[k] + mgr[k, 0] * state
    state = jnp.zeros((2, Z), F32)
    for k in reversed(range(ny)):
        from_right = jnp.where(my == k, state, from_right)
        state = partial[k] + mgr[k, 0] * state
    lanes = lax.broadcasted_iota(jnp.int32, (2, Z), 1)
    states = jnp.concatenate(
        [jnp.where(lanes < I, from_left, from_right), jnp.zeros((6, Z), F32)], axis=0)
    states = jnp.transpose(states)
    odd = lax.rem(lax.broadcasted_iota(jnp.int32, (I, Z), 1), 2) == 1
    left_state = jnp.where(odd, states[0:I, 1:2], states[0:I, 0:1])
    right_state = jnp.where(odd, states[I:2 * I, 1:2], states[I:2 * I, 0:1])
    jump = jump + wide[0:I, :] * right_state + wide[I:2 * I, :] * left_state
    for m in range(MODES):
        ls[m:m + 1, 0:2 * J] = jnp.sum(weights[m] * jump[:, 0:2 * J], axis=0, keepdims=True)

    def push_loads(k, _):
        peer = lax.rem(mx + k, nx)
        pltpu.make_async_remote_copy(
            src_ref=ls, dst_ref=lr.at[mx], send_sem=push_send.at[6], recv_sem=push_recv.at[6],
            device_id=(peer, my), device_id_type=MESH).start()
        return 0

    ls[:, 2 * J:] = jnp.zeros((MODES, Z - 2 * J), F32)
    lax.fori_loop(1, nx, push_loads, 0)
    lr[mx] = ls[...]

    arrived(lr, 6)
    total = lr[0]
    for k in range(1, nx):
        total = total + lr[k]
    fold = lax.broadcasted_iota(jnp.int32, (Z, J), 0) // 2 == lax.broadcasted_iota(
        jnp.int32, (Z, J), 1)
    loads[...] = jnp.dot(total, fold.astype(F32), precision=lax.Precision.HIGHEST,
                         preferred_element_type=F32)

    arrived(yar, 5)
    for halo in halos:
        halo.wait_send()
    for src, slot in ((xgs, 0), (xos, 1), (xas, 2), (ygs, 3), (yos, 4), (yas, 5), (lr, 6), (mgr, 7),
                      (mor, 8)):
        drained(src, slot)


def finish(I, J, Z, own, from_right, from_left, states, sums, out, loads, ya, yb, rows, sem):
    ny, _, yrow, _ = states.shape
    copies = [pltpu.make_async_copy(sums, loads, sem.at[0])]
    copies[0].start()
    for s in range(ny):
        ya[s * yrow:(s + 1) * yrow, :] = states[s, 0]
        yb[s * yrow:(s + 1) * yrow, :] = states[s, 1]
    for c in range(I // 8):
        a = ya[8 * c:8 * c + 8, :]
        b = yb[8 * c:8 * c + 8, :]
        for j in range(J):
            part = pl.ds(j * I + 8 * c, 8)
            rows[pl.ds(8 * c * J + j, 8, stride=J), :] = (
                own[part, :] + from_right[part, :] * b + from_left[part, :] * a)
        cells = pl.ds(8 * c * J, 8 * J)
        copies.append(pltpu.make_async_copy(rows.at[cells, :], out.at[cells, :], sem.at[c + 1]))
        copies[-1].start()
    for copy in copies:
        copy.wait()


def shards(nx, ny, potential, coefficient, shock_switch, x_factors, y_factors, wing_lead, wing_chord,
           panel_mode):
    I, J, Z = potential.shape
    cells = I * J
    xrow, yrow = J // nx, I // ny
    any_space = pl.BlockSpec(memory_space=pl.ANY)
    vmem = pl.BlockSpec(memory_space=pltpu.VMEM)
    block = pltpu.VMEM((cells, Z), F32)
    face = pltpu.VMEM((I, Z), F32)
    scratch = [
        pltpu.VMEM((cells + 3 * J, Z), F32),
        block,
        pltpu.VMEM((cells, Z), jnp.int32),
        pltpu.VMEM((2 * cells, Z), F32),
        pltpu.VMEM((2 * cells, Z), F32),
    ] + [block] * 12 + [face] * 4 + [
        pltpu.VMEM((2 * J, Z), F32),
        pltpu.VMEM((J, Z), F32),
        face,
    ]
    for n, rows in ((nx, xrow), (ny, yrow)):
        for members in (3, 2, 2):
            scratch += [pltpu.VMEM((n, members, rows, Z), F32)] * 2
    scratch.pop()
    scratch += [
        pltpu.VMEM((MODES, Z), F32),
        pltpu.VMEM((nx, MODES, Z), F32),
        pltpu.VMEM((2, 2, Z), F32),
        pltpu.VMEM((ny, 2, 2, Z), F32),
        pltpu.VMEM((2, Z), F32),
        pltpu.VMEM((ny, 2, Z), F32),
        pltpu.VMEM((2 * I + 2 * J * MODES, Z), F32),
        pltpu.VMEM((1, J), jnp.int32),
        pltpu.VMEM((1, J), jnp.int32),
        pltpu.VMEM((J, I), jnp.int32),
        pltpu.SemaphoreType.DMA((8,)),
        pltpu.SemaphoreType.DMA((4,)),
        pltpu.SemaphoreType.DMA((4,)),
        pltpu.SemaphoreType.DMA((9,)),
        pltpu.SemaphoreType.DMA((9,)),
    ]
    own, from_right, from_left, states, sums = pl.pallas_call(
        functools.partial(kernel, nx, ny, I, J, Z),
        out_shape=(
            block,
            block,
            block,
            pltpu.VMEM((ny, 2, yrow, Z), F32),
            pltpu.VMEM((MODES, J), F32),
        ),
        in_specs=[any_space] * 8,
        out_specs=(vmem,) * 5,
        scratch_shapes=scratch,
        compiler_params=pltpu.CompilerParams(
            collective_id=0, has_side_effects=True, vmem_limit_bytes=60 * 1024 * 1024),
        name="factored_step",
    )(
        potential.reshape(cells, Z),
        coefficient.reshape(cells, Z),
        shock_switch.reshape(cells, Z),
        x_factors.reshape(2 * cells, Z),
        y_factors.reshape(2 * cells, Z),
        wing_lead.reshape(1, J),
        wing_chord.reshape(1, J),
        panel_mode.T,
    )
    correction, loads = pl.pallas_call(
        functools.partial(finish, I, J, Z),
        out_shape=(
            jax.ShapeDtypeStruct((cells, Z), F32),
            jax.ShapeDtypeStruct((MODES, J), F32),
        ),
        in_specs=[vmem] * 5,
        out_specs=(any_space, any_space),
        scratch_shapes=[face, face, block, pltpu.SemaphoreType.DMA((I // 8 + 1,))],
        compiler_params=pltpu.CompilerParams(vmem_limit_bytes=4 * 1024 * 1024),
        name="finish",
    )(own, from_right, from_left, states, sums)
    return correction.reshape(I, J, Z), loads


def solution(mesh):
    placed = (
        P("gx", "gy", None),
        P("gx", "gy", None),
        P("gx", "gy", None),
        P(None, "gx", "gy", None),
        P(None, "gx", "gy", None),
        P("gy"),
        P("gy"),
        P("gx", "gy"),
    )
    return jax.shard_map(
        functools.partial(shards, mesh.shape["gx"], mesh.shape["gy"]),
        mesh=mesh,
        in_specs=placed,
        out_specs=(P("gx", "gy", None), P(None, "gy")),
        check_vma=False,
    )
```

```python
import functools

import jax
import jax.numpy as jnp
from jax import lax
from jax.experimental import pallas as pl
from jax.experimental.pallas import tpu as pltpu
from jax.sharding import PartitionSpec as P

MODES = 2
MESH = pl.DeviceIdType.MESH
F32 = jnp.float32


def far_first(parts):
    spans = [()]
    for size in parts:
        spans = [span + (step,) for span in spans for step in range(size)]

    def hops(span):
        return sum(min(step, size - step) for step, size in zip(span, parts))

    return sorted(spans[1:], key=lambda span: (-hops(span), span))


def moved(me, span, parts):
    place, scale = 0, 1
    for step, size in reversed(list(zip(span, parts))):
        place += lax.rem(lax.rem(me // scale, size) + step, size) * scale
        scale *= size
    return place


def complement(ratio):
    return jnp.sqrt(1.0 - ratio * ratio)


def kernel(nx, ny, I, J, Z, *refs):
    (pot, coef, switch, xf, yf, lead_hbm, chord_hbm, mode_hbm, ycb, ygb, ycc, yar, loads,
     p, cf, sw, xr, yr, xq, xs, xg, xo,
     to, tg, tc, yr0, ysc, yr1, ys1, yfw,
     face_hi, face_lo, halo_lo, halo_hi, halo_prev, halo_next, strip,
     xgs, xgr, xos, xor_, xas, xar, ygs, ygr, yos, yor, yas, ls, lr,
     mgs, mgr, mos, mor, wide, lead, chord, mode,
     load_sem, halo_send, halo_recv, push_send, push_recv) = refs
    mx = lax.axis_index("gx")
    my = lax.axis_index("gy")
    xrow, yrow = J // nx, I // ny
    xparts, yparts = (nx // 4, 4), (ny // 2, 2)
    U = 8

    barrier = pltpu.get_barrier_semaphore()

    for x_span, y_span in zip(far_first(xparts), far_first(yparts)):
        for device in ((moved(mx, x_span, xparts), my), (mx, moved(my, y_span, yparts))):
            pl.semaphore_signal(barrier, inc=1, device_id=device, device_id_type=MESH)

    load_p = pltpu.make_async_copy(pot, p.at[pl.ds(2 * J, I * J), :], load_sem.at[0])
    load_x = pltpu.make_async_copy(xf, xr, load_sem.at[1])
    load_c = pltpu.make_async_copy(coef, cf, load_sem.at[2])
    load_s = pltpu.make_async_copy(switch, sw, load_sem.at[3])
    load_y = pltpu.make_async_copy(yf, yr, load_sem.at[4])
    load_w = [pltpu.make_async_copy(src, dst, load_sem.at[slot]) for src, dst, slot in (
        (lead_hbm, lead, 5), (chord_hbm, chord, 6), (mode_hbm, mode, 7))]
    load_p.start()
    load_x.start()

    def push(src, dst, along_x, slot, same=False):
        me, parts = (mx, xparts) if along_x else (my, yparts)

        for span in far_first(parts):
            peer = moved(me, span, parts)
            pltpu.make_async_remote_copy(
                src_ref=src if same else src.at[peer],
                dst_ref=dst.at[me],
                send_sem=push_send.at[slot],
                recv_sem=push_recv.at[slot],
                device_id=(peer, my) if along_x else (mx, peer),
                device_id_type=MESH,
            ).start()

    def arrived(dst, slot):
        part = dst.at[pl.ds(0, dst.shape[0] - 1)]
        pltpu.make_async_copy(part, part, push_recv.at[slot]).wait()

    def drained(src, slot):
        part = src.at[pl.ds(0, src.shape[0] - 1)]
        pltpu.make_async_copy(part, part, push_send.at[slot]).wait()

    def at(ref, index, rows):
        return ref[pl.ds(pl.multiple_of(index * rows, 8), rows), :]

    def put(ref, index, rows, value):
        ref[pl.ds(pl.multiple_of(index * rows, 8), rows), :] = value

    def pack(dst, member, value, rows):
        total = value.shape[0]
        strip[0:total, :] = value
        for s in range(total // rows):
            dst[s, member] = strip[s * rows:(s + 1) * rows, :]

    row = lax.broadcasted_iota(jnp.int32, (J, Z), 0)
    lane = lax.broadcasted_iota(jnp.int32, (J, Z), 1)
    row8 = lax.broadcasted_iota(jnp.int32, (8, Z), 0)

    zero_line = jnp.zeros((J, Z), F32)
    pl.semaphore_wait(barrier, nx + ny - 2)

    def neighbour(src, dst, slot, device):
        return pltpu.make_async_remote_copy(
            src_ref=src, dst_ref=dst, send_sem=halo_send.at[slot], recv_sem=halo_recv.at[slot],
            device_id=device, device_id_type=MESH)

    left, right = lax.rem(mx + nx - 1, nx), lax.rem(mx + 1, nx)
    down, up = lax.rem(my + ny - 1, ny), lax.rem(my + 1, ny)
    halos = (
        neighbour(pot.at[pl.ds((I - 2) * J, 2 * J), :], halo_prev, 0, (right, my)),
        neighbour(pot.at[pl.ds(0, J), :], halo_next, 1, (left, my)),
        neighbour(face_hi, halo_lo, 2, (mx, up)),
        neighbour(face_lo, halo_hi, 3, (mx, down)),
    )
    for halo in halos[:2]:
        halo.start()
    p[0:J, :] = zero_line
    p[J:2 * J, :] = zero_line
    p[(I + 2) * J:(I + 3) * J, :] = zero_line
    load_p.wait()
    face_hi[...] = p[pl.ds(2 * J + J - 1, I, stride=J), :]
    face_lo[...] = p[pl.ds(2 * J, I, stride=J), :]
    for halo in halos[2:]:
        halo.start()
    for load in [load_c, load_s, load_y] + load_w:
        load.start()

    pair = lax.broadcasted_iota(jnp.int32, (I, Z), 1) // 2

    def pick(value, j, kept):
        return jnp.where(pair == j, pltpu.roll(value, lax.rem(2 * j + Z // 2 + 1, Z), 1), kept)

    def planes(upper, lower):
        turned = jnp.transpose(jnp.concatenate([upper, lower], axis=0))
        return turned[Z // 2 - 1:Z // 2 + 1]

    load_x.wait()

    def gain_forward(c, gain):
        for u in range(U):
            i = c * U + u
            ratio = at(xr, i, J)
            put(xq, i, J, 0.25 * complement(ratio))
            gain = ratio * gain
            put(xg, i, J, gain)
        return gain

    x_gain = lax.fori_loop(0, I // U, gain_forward, jnp.ones((J, Z), F32))

    def gain_backward(c, carry):
        gain, cross = carry
        for u in range(U):
            i = I - 1 - (c * U + u)
            ratio = at(xr, I + i, J)
            scale = complement(ratio)
            put(xs, i, J, scale)
            gain = ratio * gain
            cross = ratio * cross + scale * at(xg, i, J)
            tg[pl.ds(i, J, stride=I), :] = gain
            tc[pl.ds(i, J, stride=I), :] = cross
        return gain, cross

    x_back, x_cross = lax.fori_loop(
        0, I // U, gain_backward, (jnp.ones((J, Z), F32), jnp.zeros((J, Z), F32)))
    pack(xgs, 0, x_gain, xrow)
    pack(xgs, 1, x_back, xrow)
    pack(xgs, 2, x_cross, xrow)

    push(xgs, xgr, True, 0)

    load_c.wait()
    load_s.wait()

    def forcing(c, _):
        rows = [at(p, c * 4 + d, J) for d in range(7)]
        for u in range(4):
            i = c * 4 + u
            before2, before, center, after = rows[u:u + 4]
            twice = center + center
            second = jnp.where(at(sw, i, J) == 1, (center - 2.0 * before) + before2,
                               (after - twice) + before)
            span = jnp.where(row == 0, 0.0, pltpu.roll(center, 1, 0)) + jnp.where(
                row == J - 1, 0.0, pltpu.roll(center, J - 1, 0))
            normal = jnp.where(lane == 0, 0.0, pltpu.roll(center, 1, 1)) + jnp.where(
                lane == Z - 1, 0.0, pltpu.roll(center, Z - 1, 1))
            residual = at(cf, i, J) * second + (span - twice) + (normal - twice)
            put(xo, i, J, at(xq, i, J) * residual)
        return 0

    lax.fori_loop(0, I // 4, forcing, 0)

    for halo in halos:
        halo.wait_recv()

    before = jnp.where(mx == 0, 0.0, halo_prev[J:2 * J, :])
    before2 = jnp.where(mx == 0, 0.0, halo_prev[0:J, :])
    after = jnp.where(mx == nx - 1, 0.0, halo_next[...])
    first = jnp.where(at(sw, 0, J) == 1, before2 - 2.0 * before, before)
    second = jnp.where(at(sw, 1, J) == 1, before, 0.0)
    last = jnp.where(at(sw, I - 1, J) == 1, 0.0, after)
    for i, term in ((0, first), (1, second), (I - 1, last)):
        put(xo, i, J, at(xo, i, J) + at(xq, i, J) * (at(cf, i, J) * term))
    low = jnp.logical_and(row8 == 0, my > 0)
    high = jnp.logical_and(row8 == 7, my < ny - 1)

    def sweep_forward(c, carry):
        head, body, tail = carry
        low8 = at(halo_lo, c, U)
        high8 = at(halo_hi, c, U)
        for u in range(U):
            base = pl.multiple_of((c * U + u) * J, 8)
            r = xr[pl.ds(base, J), :]
            f = xo[pl.ds(base, J), :]
            q0 = xq[pl.ds(base, 8), :]
            q3 = xq[pl.ds(base + J - 8, 8), :]
            head = r[0:8] * head + (f[0:8] + q0 * jnp.where(low, low8[u:u + 1], 0.0))
            body = r[8:J - 8] * body + f[8:J - 8]
            tail = r[J - 8:] * tail + (f[J - 8:] + q3 * jnp.where(high, high8[u:u + 1], 0.0))
            xo[pl.ds(base, 8), :] = head
            xo[pl.ds(base + 8, J - 16), :] = body
            xo[pl.ds(base + J - 8, 8), :] = tail
        return head, body, tail

    head, body, tail = lax.fori_loop(
        0, I // U, sweep_forward,
        (jnp.zeros((8, Z), F32), jnp.zeros((J - 16, Z), F32), jnp.zeros((8, Z), F32)))

    def sweep_backward(c, state):
        for u in range(U):
            i = I - 1 - (c * U + u)
            state = at(xr, I + i, J) * state + at(xs, i, J) * at(xo, i, J)
            to[pl.ds(i, J, stride=I), :] = state
        return state

    x_first = lax.fori_loop(0, I // U, sweep_backward, jnp.zeros((J, Z), F32))
    pack(xos, 0, jnp.concatenate([head, body, tail], axis=0), xrow)
    pack(xos, 1, x_first, xrow)
    push(xos, xor_, True, 1)

    load_y.wait()

    def span_forward(c, gain):
        for u in range(2):
            j = c * 2 + u
            ratio = yr[pl.ds(j, I, stride=J), :]
            scale = complement(ratio)
            put(yr0, j, I, ratio)
            put(tg, j, I, scale * at(tg, j, I))
            put(tc, j, I, scale * at(tc, j, I))
            put(to, j, I, scale * at(to, j, I))
            gain = ratio * gain
            put(ysc, j, I, gain)
        return gain

    y_gain = lax.fori_loop(0, J // 2, span_forward, jnp.ones((I, Z), F32))

    def chain(gains, sums, gr, sr, answers, mine, me, n, rows):
        gr[me] = gains[me]
        sr[me] = sums[me]
        state = jnp.zeros((rows, Z), F32)
        partial = []
        for k in range(n):
            answers[k, 0] = state
            partial.append(sr[k, 1] + gr[k, 2] * state)
            state = sr[k, 0] + gr[k, 0] * state
        state = jnp.zeros((rows, Z), F32)
        for k in reversed(range(n)):
            answers[k, 1] = state
            state = partial[k] + gr[k, 1] * state
        mine[me] = answers[me]

    arrived(xgr, 0)
    arrived(xor_, 1)
    chain(xgs, xos, xgr, xor_, xas, xar, mx, nx, xrow)
    push(xas, xar, True, 2)

    def span_backward(c, carry):
        gain, cross, gains2, crosses2 = carry
        for u in range(2):
            j = J - 1 - (c * 2 + u)
            ratio = yr[pl.ds(I * J + j, I, stride=J), :]
            scale = complement(ratio)
            put(yr1, j, I, ratio)
            put(ys1, j, I, scale)
            gain = ratio * gain
            cross = ratio * cross + scale * at(ysc, j, I)
            put(ygb, j, I, gain)
            put(ycc, j, I, cross)
            gains2 = pick(gain, j, gains2)
            crosses2 = pick(cross, j, crosses2)
        return gain, cross, gains2, crosses2

    zero_face = jnp.zeros((I, Z), F32)
    y_back, y_cross, gains2, crosses2 = lax.fori_loop(
        0, J // 2, span_backward, (jnp.ones((I, Z), F32), zero_face, zero_face, zero_face))
    wide[0:I, :] = gains2
    wide[I:2 * I, :] = crosses2
    pack(ygs, 0, y_gain, yrow)
    pack(ygs, 1, y_back, yrow)
    pack(ygs, 2, y_cross, yrow)
    push(ygs, ygr, False, 3)
    mgs[0] = planes(y_gain, y_back)
    mgs[1] = planes(y_cross, y_cross)
    push(mgs, mgr, False, 7, True)

    arrived(xar, 2)

    def across(s, state):
        for t in range(xrow):
            j = s * xrow + t
            a = xar[s, 0, t:t + 1, :]
            b = xar[s, 1, t:t + 1, :]
            source = at(to, j, I) + at(tg, j, I) * b + at(tc, j, I) * a
            state = at(yr0, j, I) * state + source
            put(yfw, j, I, state)
        return state

    y_last = lax.fori_loop(0, nx, across, jnp.zeros((I, Z), F32))

    def back(c, state):
        for u in range(2):
            j = J - 1 - (c * 2 + u)
            state = at(yr1, j, I) * state + at(ys1, j, I) * at(yfw, j, I)
            put(ycb, j, I, state)
        return state

    y_first = lax.fori_loop(0, J // 2, back, jnp.zeros((I, Z), F32))
    mos[...] = planes(y_last, y_first)
    push(mos, mor, False, 8, True)
    pack(yos, 0, y_last, yrow)
    pack(yos, 1, y_first, yrow)
    push(yos, yor, False, 4)


    def own_planes(j, kept):
        return pick(p[pl.ds(2 * J + j, I, stride=J), :] + at(ycb, j, I), j, kept)

    jump = lax.fori_loop(0, J, own_planes, zero_face)

    for load in load_w:
        load.wait()
    stream = mx * I + lax.broadcasted_iota(jnp.int32, (J, I), 1)
    begin = jnp.transpose(jnp.broadcast_to(lead[...], (8, J)))[:, 0:1]
    length = jnp.transpose(jnp.broadcast_to(chord[...], (8, J)))[:, 0:1]
    onwing = jnp.logical_and(stream >= begin, stream < begin + length)
    weight = jnp.where(onwing, 0.5 + 2.5 * stream.astype(F32) / (I * nx), 0.0) / jnp.sqrt(
        length.astype(F32))
    weights = []
    for m in range(MODES):
        own = jnp.concatenate(
            [jnp.where(mode[...] == m, weight, 0.0), jnp.zeros((J, Z - I), F32)], axis=1)
        rows = 2 * I + m * 2 * J
        wide[pl.ds(rows, J, stride=2), :] = -own
        wide[pl.ds(rows + 1, J, stride=2), :] = own
        weights.append(jnp.transpose(wide[rows:rows + 2 * J, :])[0:I])

    arrived(ygr, 3)
    arrived(yor, 4)
    chain(ygs, yos, ygr, yor, yas, yar, my, ny, yrow)
    push(yas, yar, False, 5)

    arrived(mgr, 7)
    arrived(mor, 8)
    mgr[my] = mgs[...]
    mor[my] = mos[...]
    state = jnp.zeros((2, Z), F32)
    from_left = from_right = state
    partial = []
    for k in range(ny):
        from_left = jnp.where(my == k, state, from_left)
        partial.append(mor[k] + mgr[k, 1] * pltpu.roll(state, I, 1))
        state = mor[k] + mgr[k, 0] * state
    state = jnp.zeros((2, Z), F32)
    for k in reversed(range(ny)):
        from_right = jnp.where(my == k, state, from_right)
        state = partial[k] + mgr[k, 0] * state
    lanes = lax.broadcasted_iota(jnp.int32, (2, Z), 1)
    states = jnp.concatenate(
        [jnp.where(lanes < I, from_left, from_right), jnp.zeros((6, Z), F32)], axis=0)
    states = jnp.transpose(states)
    odd = lax.rem(lax.broadcasted_iota(jnp.int32, (I, Z), 1), 2) == 1
    left_state = jnp.where(odd, states[0:I, 1:2], states[0:I, 0:1])
    right_state = jnp.where(odd, states[I:2 * I, 1:2], states[I:2 * I, 0:1])
    jump = jump + wide[0:I, :] * right_state + wide[I:2 * I, :] * left_state
    for m in range(MODES):
        ls[m:m + 1, 0:2 * J] = jnp.sum(weights[m] * jump[:, 0:2 * J], axis=0, keepdims=True)

    ls[:, 2 * J:] = jnp.zeros((MODES, Z - 2 * J), F32)
    push(ls, lr, True, 6, True)
    lr[mx] = ls[...]

    arrived(lr, 6)
    total = lr[0]
    for k in range(1, nx):
        total = total + lr[k]
    fold = lax.broadcasted_iota(jnp.int32, (Z, J), 0) // 2 == lax.broadcasted_iota(
        jnp.int32, (Z, J), 1)
    loads[...] = jnp.dot(total, fold.astype(F32), precision=lax.Precision.HIGHEST,
                         preferred_element_type=F32)

    arrived(yar, 5)
    for halo in halos:
        halo.wait_send()
    for src, slot in ((xgs, 0), (xos, 1), (xas, 2), (ygs, 3), (yos, 4), (yas, 5), (lr, 6), (mgr, 7),
                      (mor, 8)):
        drained(src, slot)


def finish(I, J, Z, own, from_right, from_left, states, sums, out, loads, ya, yb, rows, sem):
    ny, _, yrow, _ = states.shape
    copies = [pltpu.make_async_copy(sums, loads, sem.at[0])]
    copies[0].start()
    for s in range(ny):
        ya[s * yrow:(s + 1) * yrow, :] = states[s, 0]
        yb[s * yrow:(s + 1) * yrow, :] = states[s, 1]
    for c in range(I // 8):
        a = ya[8 * c:8 * c + 8, :]
        b = yb[8 * c:8 * c + 8, :]
        for j in range(J):
            part = pl.ds(j * I + 8 * c, 8)
            rows[pl.ds(8 * c * J + j, 8, stride=J), :] = (
                own[part, :] + from_right[part, :] * b + from_left[part, :] * a)
        cells = pl.ds(8 * c * J, 8 * J)
        copies.append(pltpu.make_async_copy(rows.at[cells, :], out.at[cells, :], sem.at[c + 1]))
        copies[-1].start()
    for copy in copies:
        copy.wait()


def shards(nx, ny, potential, coefficient, shock_switch, x_factors, y_factors, wing_lead, wing_chord,
           panel_mode):
    I, J, Z = potential.shape
    cells = I * J
    xrow, yrow = J // nx, I // ny
    any_space = pl.BlockSpec(memory_space=pl.ANY)
    vmem = pl.BlockSpec(memory_space=pltpu.VMEM)
    block = pltpu.VMEM((cells, Z), F32)
    face = pltpu.VMEM((I, Z), F32)
    scratch = [
        pltpu.VMEM((cells + 3 * J, Z), F32),
        block,
        pltpu.VMEM((cells, Z), jnp.int32),
        pltpu.VMEM((2 * cells, Z), F32),
        pltpu.VMEM((2 * cells, Z), F32),
    ] + [block] * 12 + [face] * 4 + [
        pltpu.VMEM((2 * J, Z), F32),
        pltpu.VMEM((J, Z), F32),
        face,
    ]
    for n, rows in ((nx, xrow), (ny, yrow)):
        for members in (3, 2, 2):
            scratch += [pltpu.VMEM((n, members, rows, Z), F32)] * 2
    scratch.pop()
    scratch += [
        pltpu.VMEM((MODES, Z), F32),
        pltpu.VMEM((nx, MODES, Z), F32),
        pltpu.VMEM((2, 2, Z), F32),
        pltpu.VMEM((ny, 2, 2, Z), F32),
        pltpu.VMEM((2, Z), F32),
        pltpu.VMEM((ny, 2, Z), F32),
        pltpu.VMEM((2 * I + 2 * J * MODES, Z), F32),
        pltpu.VMEM((1, J), jnp.int32),
        pltpu.VMEM((1, J), jnp.int32),
        pltpu.VMEM((J, I), jnp.int32),
        pltpu.SemaphoreType.DMA((8,)),
        pltpu.SemaphoreType.DMA((4,)),
        pltpu.SemaphoreType.DMA((4,)),
        pltpu.SemaphoreType.DMA((9,)),
        pltpu.SemaphoreType.DMA((9,)),
    ]
    own, from_right, from_left, states, sums = pl.pallas_call(
        functools.partial(kernel, nx, ny, I, J, Z),
        out_shape=(
            block,
            block,
            block,
            pltpu.VMEM((ny, 2, yrow, Z), F32),
            pltpu.VMEM((MODES, J), F32),
        ),
        in_specs=[any_space] * 8,
        out_specs=(vmem,) * 5,
        scratch_shapes=scratch,
        compiler_params=pltpu.CompilerParams(
            collective_id=0, has_side_effects=True, vmem_limit_bytes=60 * 1024 * 1024),
        name="factored_step",
    )(
        potential.reshape(cells, Z),
        coefficient.reshape(cells, Z),
        shock_switch.reshape(cells, Z),
        x_factors.reshape(2 * cells, Z),
        y_factors.reshape(2 * cells, Z),
        wing_lead.reshape(1, J),
        wing_chord.reshape(1, J),
        panel_mode.T,
    )
    correction, loads = pl.pallas_call(
        functools.partial(finish, I, J, Z),
        out_shape=(
            jax.ShapeDtypeStruct((cells, Z), F32),
            jax.ShapeDtypeStruct((MODES, J), F32),
        ),
        in_specs=[vmem] * 5,
        out_specs=(any_space, any_space),
        scratch_shapes=[face, face, block, pltpu.SemaphoreType.DMA((I // 8 + 1,))],
        compiler_params=pltpu.CompilerParams(vmem_limit_bytes=4 * 1024 * 1024),
        name="finish",
    )(own, from_right, from_left, states, sums)
    return correction.reshape(I, J, Z), loads


def solution(mesh):
    placed = (
        P("gx", "gy", None),
        P("gx", "gy", None),
        P("gx", "gy", None),
        P(None, "gx", "gy", None),
        P(None, "gx", "gy", None),
        P("gy"),
        P("gy"),
        P("gx", "gy"),
    )
    return jax.shard_map(
        functools.partial(shards, mesh.shape["gx"], mesh.shape["gy"]),
        mesh=mesh,
        in_specs=placed,
        out_specs=(P("gx", "gy", None), P(None, "gy")),
        check_vma=False,
    )
```

```python
import functools

import jax
import jax.numpy as jnp
from jax import lax
from jax.experimental import pallas as pl
from jax.experimental.pallas import tpu as pltpu
from jax.sharding import PartitionSpec as P

MODES = 2
MESH = pl.DeviceIdType.MESH
F32 = jnp.float32


def far_first(parts):
    spans = [()]
    for size in parts:
        spans = [span + (step,) for span in spans for step in range(size)]

    def hops(span):
        return sum(min(step, size - step) for step, size in zip(span, parts))

    return sorted(spans[1:], key=lambda span: (-hops(span), span))


def moved(me, span, parts):
    place, scale = 0, 1
    for step, size in reversed(list(zip(span, parts))):
        place += lax.rem(lax.rem(me // scale, size) + step, size) * scale
        scale *= size
    return place


def complement(ratio):
    return jnp.sqrt(1.0 - ratio * ratio)


def kernel(nx, ny, I, J, Z, *refs):
    (pot, coef, switch, xf, yf, lead_hbm, chord_hbm, mode_hbm, ycb, ygb, ycc, yar, loads,
     p, cf, sw, xr, yr, xq, xs, xg, xo,
     to, tg, tc, yr0, ysc, yr1, ys1, yfw,
     face_hi, face_lo, halo_lo, halo_hi, halo_prev, halo_next, strip,
     xgs, xgr, xos, xor_, xas, xar, ygs, ygr, yos, yor, yas, ls, lr,
     mgs, mgr, mos, mor, wide, lead, chord, mode,
     load_sem, halo_send, halo_recv, push_send, push_recv) = refs
    mx = lax.axis_index("gx")
    my = lax.axis_index("gy")
    xrow, yrow = J // nx, I // ny
    xparts, yparts = (nx // 4, 4), (ny // 2, 2)
    U = 8

    barrier = pltpu.get_barrier_semaphore()

    for x_span, y_span in zip(far_first(xparts), far_first(yparts)):
        for device in ((moved(mx, x_span, xparts), my), (mx, moved(my, y_span, yparts))):
            pl.semaphore_signal(barrier, inc=1, device_id=device, device_id_type=MESH)

    load_p = pltpu.make_async_copy(pot, p.at[pl.ds(2 * J, I * J), :], load_sem.at[0])
    load_x = pltpu.make_async_copy(xf, xr, load_sem.at[1])
    load_c = pltpu.make_async_copy(coef, cf, load_sem.at[2])
    load_s = pltpu.make_async_copy(switch, sw, load_sem.at[3])
    load_y = pltpu.make_async_copy(yf, yr, load_sem.at[4])
    load_w = [pltpu.make_async_copy(src, dst, load_sem.at[slot]) for src, dst, slot in (
        (lead_hbm, lead, 5), (chord_hbm, chord, 6), (mode_hbm, mode, 7))]
    load_p.start()
    load_x.start()

    def push(src, dst, along_x, slot, same=False):
        me, parts = (mx, xparts) if along_x else (my, yparts)

        for span in far_first(parts):
            peer = moved(me, span, parts)
            pltpu.make_async_remote_copy(
                src_ref=src if same else src.at[peer],
                dst_ref=dst.at[me],
                send_sem=push_send.at[slot],
                recv_sem=push_recv.at[slot],
                device_id=(peer, my) if along_x else (mx, peer),
                device_id_type=MESH,
            ).start()

    def arrived(dst, slot):
        part = dst.at[pl.ds(0, dst.shape[0] - 1)]
        pltpu.make_async_copy(part, part, push_recv.at[slot]).wait()

    def drained(src, slot):
        part = src.at[pl.ds(0, src.shape[0] - 1)]
        pltpu.make_async_copy(part, part, push_send.at[slot]).wait()

    def at(ref, index, rows):
        return ref[pl.ds(pl.multiple_of(index * rows, 8), rows), :]

    def put(ref, index, rows, value):
        ref[pl.ds(pl.multiple_of(index * rows, 8), rows), :] = value

    def pack(dst, member, value, rows):
        total = value.shape[0]
        strip[0:total, :] = value
        for s in range(total // rows):
            dst[s, member] = strip[s * rows:(s + 1) * rows, :]

    row = lax.broadcasted_iota(jnp.int32, (J, Z), 0)
    lane = lax.broadcasted_iota(jnp.int32, (J, Z), 1)
    row8 = lax.broadcasted_iota(jnp.int32, (8, Z), 0)

    zero_line = jnp.zeros((J, Z), F32)
    pl.semaphore_wait(barrier, nx + ny - 2)

    def neighbour(src, dst, slot, device):
        return pltpu.make_async_remote_copy(
            src_ref=src, dst_ref=dst, send_sem=halo_send.at[slot], recv_sem=halo_recv.at[slot],
            device_id=device, device_id_type=MESH)

    left, right = lax.rem(mx + nx - 1, nx), lax.rem(mx + 1, nx)
    down, up = lax.rem(my + ny - 1, ny), lax.rem(my + 1, ny)
    halos = (
        neighbour(pot.at[pl.ds((I - 2) * J, 2 * J), :], halo_prev, 0, (right, my)),
        neighbour(pot.at[pl.ds(0, J), :], halo_next, 1, (left, my)),
        neighbour(face_hi, halo_lo, 2, (mx, up)),
        neighbour(face_lo, halo_hi, 3, (mx, down)),
    )
    for halo in halos[:2]:
        halo.start()
    p[0:J, :] = zero_line
    p[J:2 * J, :] = zero_line
    p[(I + 2) * J:(I + 3) * J, :] = zero_line
    load_p.wait()
    face_hi[...] = p[pl.ds(2 * J + J - 1, I, stride=J), :]
    face_lo[...] = p[pl.ds(2 * J, I, stride=J), :]
    for halo in halos[2:]:
        halo.start()
    for load in [load_c, load_s, load_y] + load_w:
        load.start()

    pair = lax.broadcasted_iota(jnp.int32, (I, Z), 1) // 2

    def pick(value, j, kept):
        return jnp.where(pair == j, pltpu.roll(value, lax.rem(2 * j + Z // 2 + 1, Z), 1), kept)

    def planes(upper, lower):
        turned = jnp.transpose(jnp.concatenate([upper, lower], axis=0))
        return turned[Z // 2 - 1:Z // 2 + 1]

    load_x.wait()

    def gain_forward(c, gain):
        for u in range(U):
            i = c * U + u
            ratio = at(xr, i, J)
            put(xq, i, J, 0.25 * complement(ratio))
            gain = ratio * gain
            put(xg, i, J, gain)
        return gain

    x_gain = lax.fori_loop(0, I // U, gain_forward, jnp.ones((J, Z), F32))

    def gain_backward(c, carry):
        gain, cross = carry
        for u in range(U):
            i = I - 1 - (c * U + u)
            ratio = at(xr, I + i, J)
            scale = complement(ratio)
            put(xs, i, J, scale)
            gain = ratio * gain
            cross = ratio * cross + scale * at(xg, i, J)
            tg[pl.ds(i, J, stride=I), :] = gain
            tc[pl.ds(i, J, stride=I), :] = cross
        return gain, cross

    x_back, x_cross = lax.fori_loop(
        0, I // U, gain_backward, (jnp.ones((J, Z), F32), jnp.zeros((J, Z), F32)))
    pack(xgs, 0, x_gain, xrow)
    pack(xgs, 1, x_back, xrow)
    pack(xgs, 2, x_cross, xrow)

    push(xgs, xgr, True, 0)

    load_c.wait()
    load_s.wait()

    def forcing(c, _):
        rows = [at(p, c * 4 + d, J) for d in range(7)]
        for u in range(4):
            i = c * 4 + u
            before2, before, center, after = rows[u:u + 4]
            twice = center + center
            second = jnp.where(at(sw, i, J) == 1, (center - 2.0 * before) + before2,
                               (after - twice) + before)
            span = jnp.where(row == 0, 0.0, pltpu.roll(center, 1, 0)) + jnp.where(
                row == J - 1, 0.0, pltpu.roll(center, J - 1, 0))
            normal = jnp.where(lane == 0, 0.0, pltpu.roll(center, 1, 1)) + jnp.where(
                lane == Z - 1, 0.0, pltpu.roll(center, Z - 1, 1))
            residual = at(cf, i, J) * second + (span - twice) + (normal - twice)
            put(xo, i, J, at(xq, i, J) * residual)
        return 0

    lax.fori_loop(0, I // 4, forcing, 0)

    for halo in halos:
        halo.wait_recv()

    before = jnp.where(mx == 0, 0.0, halo_prev[J:2 * J, :])
    before2 = jnp.where(mx == 0, 0.0, halo_prev[0:J, :])
    after = jnp.where(mx == nx - 1, 0.0, halo_next[...])
    first = jnp.where(at(sw, 0, J) == 1, before2 - 2.0 * before, before)
    second = jnp.where(at(sw, 1, J) == 1, before, 0.0)
    last = jnp.where(at(sw, I - 1, J) == 1, 0.0, after)
    for i, term in ((0, first), (1, second), (I - 1, last)):
        put(xo, i, J, at(xo, i, J) + at(xq, i, J) * (at(cf, i, J) * term))
    low = jnp.logical_and(row8 == 0, my > 0)
    high = jnp.logical_and(row8 == 7, my < ny - 1)

    def sweep_forward(c, carry):
        head, body, tail = carry
        low8 = at(halo_lo, c, U)
        high8 = at(halo_hi, c, U)
        for u in range(U):
            base = pl.multiple_of((c * U + u) * J, 8)
            r = xr[pl.ds(base, J), :]
            f = xo[pl.ds(base, J), :]
            q0 = xq[pl.ds(base, 8), :]
            q3 = xq[pl.ds(base + J - 8, 8), :]
            head = r[0:8] * head + (f[0:8] + q0 * jnp.where(low, low8[u:u + 1], 0.0))
            body = r[8:J - 8] * body + f[8:J - 8]
            tail = r[J - 8:] * tail + (f[J - 8:] + q3 * jnp.where(high, high8[u:u + 1], 0.0))
            xo[pl.ds(base, 8), :] = head
            xo[pl.ds(base + 8, J - 16), :] = body
            xo[pl.ds(base + J - 8, 8), :] = tail
        return head, body, tail

    head, body, tail = lax.fori_loop(
        0, I // U, sweep_forward,
        (jnp.zeros((8, Z), F32), jnp.zeros((J - 16, Z), F32), jnp.zeros((8, Z), F32)))

    def sweep_backward(c, state):
        for u in range(U):
            i = I - 1 - (c * U + u)
            state = at(xr, I + i, J) * state + at(xs, i, J) * at(xo, i, J)
            to[pl.ds(i, J, stride=I), :] = state
        return state

    x_first = lax.fori_loop(0, I // U, sweep_backward, jnp.zeros((J, Z), F32))
    pack(xos, 0, jnp.concatenate([head, body, tail], axis=0), xrow)
    pack(xos, 1, x_first, xrow)
    push(xos, xor_, True, 1)

    load_y.wait()

    def span_forward(c, gain):
        for u in range(2):
            j = c * 2 + u
            ratio = yr[pl.ds(j, I, stride=J), :]
            scale = complement(ratio)
            put(yr0, j, I, ratio)
            put(tg, j, I, scale * at(tg, j, I))
            put(tc, j, I, scale * at(tc, j, I))
            put(to, j, I, scale * at(to, j, I))
            gain = ratio * gain
            put(ysc, j, I, gain)
        return gain

    y_gain = lax.fori_loop(0, J // 2, span_forward, jnp.ones((I, Z), F32))

    def chain(gains, sums, gr, sr, answers, mine, me, n, rows):
        gr[me] = gains[me]
        sr[me] = sums[me]
        state = jnp.zeros((rows, Z), F32)
        partial = []
        for k in range(n):
            answers[k, 0] = state
            partial.append(sr[k, 1] + gr[k, 2] * state)
            state = sr[k, 0] + gr[k, 0] * state
        state = jnp.zeros((rows, Z), F32)
        for k in reversed(range(n)):
            answers[k, 1] = state
            state = partial[k] + gr[k, 1] * state
        mine[me] = answers[me]

    arrived(xgr, 0)
    arrived(xor_, 1)
    chain(xgs, xos, xgr, xor_, xas, xar, mx, nx, xrow)
    push(xas, xar, True, 2)

    def span_backward(c, carry):
        gain, cross, gains2, crosses2 = carry
        for u in range(2):
            j = J - 1 - (c * 2 + u)
            ratio = yr[pl.ds(I * J + j, I, stride=J), :]
            scale = complement(ratio)
            put(yr1, j, I, ratio)
            put(ys1, j, I, scale)
            gain = ratio * gain
            cross = ratio * cross + scale * at(ysc, j, I)
            put(ygb, j, I, gain)
            put(ycc, j, I, cross)
            gains2 = pick(gain, j, gains2)
            crosses2 = pick(cross, j, crosses2)
        return gain, cross, gains2, crosses2

    zero_face = jnp.zeros((I, Z), F32)
    y_back, y_cross, gains2, crosses2 = lax.fori_loop(
        0, J // 2, span_backward, (jnp.ones((I, Z), F32), zero_face, zero_face, zero_face))
    wide[0:I, :] = gains2
    wide[I:2 * I, :] = crosses2
    pack(ygs, 0, y_gain, yrow)
    pack(ygs, 1, y_back, yrow)
    pack(ygs, 2, y_cross, yrow)
    push(ygs, ygr, False, 3)
    mgs[0] = planes(y_gain, y_back)
    mgs[1] = planes(y_cross, y_cross)
    push(mgs, mgr, False, 7, True)

    arrived(xar, 2)

    def across(c, state):
        for u in range(4 * xrow):
            s, t = c * 4 + u // xrow, u % xrow
            j = c * 4 * xrow + u
            a = xar[s, 0, t:t + 1, :]
            b = xar[s, 1, t:t + 1, :]
            source = at(to, j, I) + at(tg, j, I) * b + at(tc, j, I) * a
            state = at(yr0, j, I) * state + source
            put(yfw, j, I, state)
        return state

    y_last = lax.fori_loop(0, nx // 4, across, jnp.zeros((I, Z), F32))

    def back(c, state):
        for u in range(U):
            j = J - 1 - (c * U + u)
            state = at(yr1, j, I) * state + at(ys1, j, I) * at(yfw, j, I)
            put(ycb, j, I, state)
        return state

    y_first = lax.fori_loop(0, J // U, back, jnp.zeros((I, Z), F32))
    pack(yos, 0, y_last, yrow)
    pack(yos, 1, y_first, yrow)
    push(yos, yor, False, 4)
    mos[...] = planes(y_last, y_first)
    push(mos, mor, False, 8, True)


    def own_planes(j, kept):
        return pick(p[pl.ds(2 * J + j, I, stride=J), :] + at(ycb, j, I), j, kept)

    jump = lax.fori_loop(0, J, own_planes, zero_face)

    for load in load_w:
        load.wait()
    stream = mx * I + lax.broadcasted_iota(jnp.int32, (J, I), 1)
    begin = jnp.transpose(jnp.broadcast_to(lead[...], (8, J)))[:, 0:1]
    length = jnp.transpose(jnp.broadcast_to(chord[...], (8, J)))[:, 0:1]
    onwing = jnp.logical_and(stream >= begin, stream < begin + length)
    weight = jnp.where(onwing, 0.5 + 2.5 * stream.astype(F32) / (I * nx), 0.0) / jnp.sqrt(
        length.astype(F32))
    weights = []
    for m in range(MODES):
        own = jnp.concatenate(
            [jnp.where(mode[...] == m, weight, 0.0), jnp.zeros((J, Z - I), F32)], axis=1)
        rows = 2 * I + m * 2 * J
        wide[pl.ds(rows, J, stride=2), :] = -own
        wide[pl.ds(rows + 1, J, stride=2), :] = own
        weights.append(jnp.transpose(wide[rows:rows + 2 * J, :])[0:I])

    arrived(ygr, 3)
    arrived(yor, 4)
    chain(ygs, yos, ygr, yor, yas, yar, my, ny, yrow)
    push(yas, yar, False, 5)

    arrived(mgr, 7)
    arrived(mor, 8)
    mgr[my] = mgs[...]
    mor[my] = mos[...]
    state = jnp.zeros((2, Z), F32)
    from_left = from_right = state
    partial = []
    for k in range(ny):
        from_left = jnp.where(my == k, state, from_left)
        partial.append(mor[k] + mgr[k, 1] * pltpu.roll(state, I, 1))
        state = mor[k] + mgr[k, 0] * state
    state = jnp.zeros((2, Z), F32)
    for k in reversed(range(ny)):
        from_right = jnp.where(my == k, state, from_right)
        state = partial[k] + mgr[k, 0] * state
    lanes = lax.broadcasted_iota(jnp.int32, (2, Z), 1)
    states = jnp.concatenate(
        [jnp.where(lanes < I, from_left, from_right), jnp.zeros((6, Z), F32)], axis=0)
    states = jnp.transpose(states)
    odd = lax.rem(lax.broadcasted_iota(jnp.int32, (I, Z), 1), 2) == 1
    left_state = jnp.where(odd, states[0:I, 1:2], states[0:I, 0:1])
    right_state = jnp.where(odd, states[I:2 * I, 1:2], states[I:2 * I, 0:1])
    jump = jump + wide[0:I, :] * right_state + wide[I:2 * I, :] * left_state
    for m in range(MODES):
        ls[m:m + 1, 0:2 * J] = jnp.sum(weights[m] * jump[:, 0:2 * J], axis=0, keepdims=True)

    ls[:, 2 * J:] = jnp.zeros((MODES, Z - 2 * J), F32)
    push(ls, lr, True, 6, True)
    lr[mx] = ls[...]

    arrived(lr, 6)
    total = lr[0]
    for k in range(1, nx):
        total = total + lr[k]
    fold = lax.broadcasted_iota(jnp.int32, (Z, J), 0) // 2 == lax.broadcasted_iota(
        jnp.int32, (Z, J), 1)
    loads[...] = jnp.dot(total, fold.astype(F32), precision=lax.Precision.HIGHEST,
                         preferred_element_type=F32)

    arrived(yar, 5)
    for halo in halos:
        halo.wait_send()
    for src, slot in ((xgs, 0), (xos, 1), (xas, 2), (ygs, 3), (yos, 4), (yas, 5), (lr, 6), (mgr, 7),
                      (mor, 8)):
        drained(src, slot)


def finish(I, J, Z, own, from_right, from_left, states, sums, out, loads, ya, yb, rows, sem):
    ny, _, yrow, _ = states.shape
    copies = [pltpu.make_async_copy(sums, loads, sem.at[0])]
    copies[0].start()
    for s in range(ny):
        ya[s * yrow:(s + 1) * yrow, :] = states[s, 0]
        yb[s * yrow:(s + 1) * yrow, :] = states[s, 1]
    for c in range(I // 8):
        a = ya[8 * c:8 * c + 8, :]
        b = yb[8 * c:8 * c + 8, :]
        for j in range(J):
            part = pl.ds(j * I + 8 * c, 8)
            rows[pl.ds(8 * c * J + j, 8, stride=J), :] = (
                own[part, :] + from_right[part, :] * b + from_left[part, :] * a)
        cells = pl.ds(8 * c * J, 8 * J)
        copies.append(pltpu.make_async_copy(rows.at[cells, :], out.at[cells, :], sem.at[c + 1]))
        copies[-1].start()
    for copy in copies:
        copy.wait()


def shards(nx, ny, potential, coefficient, shock_switch, x_factors, y_factors, wing_lead, wing_chord,
           panel_mode):
    I, J, Z = potential.shape
    cells = I * J
    xrow, yrow = J // nx, I // ny
    any_space = pl.BlockSpec(memory_space=pl.ANY)
    vmem = pl.BlockSpec(memory_space=pltpu.VMEM)
    block = pltpu.VMEM((cells, Z), F32)
    face = pltpu.VMEM((I, Z), F32)
    scratch = [
        pltpu.VMEM((cells + 3 * J, Z), F32),
        block,
        pltpu.VMEM((cells, Z), jnp.int32),
        pltpu.VMEM((2 * cells, Z), F32),
        pltpu.VMEM((2 * cells, Z), F32),
    ] + [block] * 12 + [face] * 4 + [
        pltpu.VMEM((2 * J, Z), F32),
        pltpu.VMEM((J, Z), F32),
        face,
    ]
    for n, rows in ((nx, xrow), (ny, yrow)):
        for members in (3, 2, 2):
            scratch += [pltpu.VMEM((n, members, rows, Z), F32)] * 2
    scratch.pop()
    scratch += [
        pltpu.VMEM((MODES, Z), F32),
        pltpu.VMEM((nx, MODES, Z), F32),
        pltpu.VMEM((2, 2, Z), F32),
        pltpu.VMEM((ny, 2, 2, Z), F32),
        pltpu.VMEM((2, Z), F32),
        pltpu.VMEM((ny, 2, Z), F32),
        pltpu.VMEM((2 * I + 2 * J * MODES, Z), F32),
        pltpu.VMEM((1, J), jnp.int32),
        pltpu.VMEM((1, J), jnp.int32),
        pltpu.VMEM((J, I), jnp.int32),
        pltpu.SemaphoreType.DMA((8,)),
        pltpu.SemaphoreType.DMA((4,)),
        pltpu.SemaphoreType.DMA((4,)),
        pltpu.SemaphoreType.DMA((9,)),
        pltpu.SemaphoreType.DMA((9,)),
    ]
    own, from_right, from_left, states, sums = pl.pallas_call(
        functools.partial(kernel, nx, ny, I, J, Z),
        out_shape=(
            block,
            block,
            block,
            pltpu.VMEM((ny, 2, yrow, Z), F32),
            pltpu.VMEM((MODES, J), F32),
        ),
        in_specs=[any_space] * 8,
        out_specs=(vmem,) * 5,
        scratch_shapes=scratch,
        compiler_params=pltpu.CompilerParams(
            collective_id=0, has_side_effects=True, vmem_limit_bytes=60 * 1024 * 1024),
        name="factored_step",
    )(
        potential.reshape(cells, Z),
        coefficient.reshape(cells, Z),
        shock_switch.reshape(cells, Z),
        x_factors.reshape(2 * cells, Z),
        y_factors.reshape(2 * cells, Z),
        wing_lead.reshape(1, J),
        wing_chord.reshape(1, J),
        panel_mode.T,
    )
    correction, loads = pl.pallas_call(
        functools.partial(finish, I, J, Z),
        out_shape=(
            jax.ShapeDtypeStruct((cells, Z), F32),
            jax.ShapeDtypeStruct((MODES, J), F32),
        ),
        in_specs=[vmem] * 5,
        out_specs=(any_space, any_space),
        scratch_shapes=[face, face, block, pltpu.SemaphoreType.DMA((I // 8 + 1,))],
        compiler_params=pltpu.CompilerParams(vmem_limit_bytes=4 * 1024 * 1024),
        name="finish",
    )(own, from_right, from_left, states, sums)
    return correction.reshape(I, J, Z), loads


def solution(mesh):
    placed = (
        P("gx", "gy", None),
        P("gx", "gy", None),
        P("gx", "gy", None),
        P(None, "gx", "gy", None),
        P(None, "gx", "gy", None),
        P("gy"),
        P("gy"),
        P("gx", "gy"),
    )
    return jax.shard_map(
        functools.partial(shards, mesh.shape["gx"], mesh.shape["gy"]),
        mesh=mesh,
        in_specs=placed,
        out_specs=(P("gx", "gy", None), P(None, "gy")),
        check_vma=False,
    )
```

```python
import functools

import jax
import jax.numpy as jnp
from jax import lax
from jax.experimental import pallas as pl
from jax.experimental.pallas import tpu as pltpu
from jax.sharding import PartitionSpec as P

MODES = 2
MESH = pl.DeviceIdType.MESH
F32 = jnp.float32


def far_first(parts):
    spans = [()]
    for size in parts:
        spans = [span + (step,) for span in spans for step in range(size)]

    def hops(span):
        return sum(min(step, size - step) for step, size in zip(span, parts))

    return sorted(spans[1:], key=lambda span: (-hops(span), span))


def moved(me, span, parts):
    place, scale = 0, 1
    for step, size in reversed(list(zip(span, parts))):
        place += lax.rem(lax.rem(me // scale, size) + step, size) * scale
        scale *= size
    return place


def complement(ratio):
    return jnp.sqrt(1.0 - ratio * ratio)


def kernel(nx, ny, I, J, Z, *refs):
    (pot, coef, switch, xf, yf, lead_hbm, chord_hbm, mode_hbm, ycb, ygb, ycc, yar, loads,
     p, cf, sw, xr, yr, xq, xs, xg, xo,
     to, tg, tc, yr0, ysc, yr1, ys1, yfw,
     face_hi, face_lo, halo_lo, halo_hi, halo_prev, halo_next, strip,
     xgs, xgr, xos, xor_, xas, xar, ygs, ygr, yos, yor, yas, ls, lr,
     mgs, mgr, mos, mor, wide, lead, chord, mode,
     load_sem, halo_send, halo_recv, push_send, push_recv) = refs
    mx = lax.axis_index("gx")
    my = lax.axis_index("gy")
    xrow, yrow = J // nx, I // ny
    xparts, yparts = (nx // 4, 4), (ny // 2, 2)
    U = 8

    barrier = pltpu.get_barrier_semaphore()

    for x_span, y_span in zip(far_first(xparts), far_first(yparts)):
        for device in ((moved(mx, x_span, xparts), my), (mx, moved(my, y_span, yparts))):
            pl.semaphore_signal(barrier, inc=1, device_id=device, device_id_type=MESH)

    load_p = pltpu.make_async_copy(pot, p.at[pl.ds(2 * J, I * J), :], load_sem.at[0])
    load_x = pltpu.make_async_copy(xf, xr, load_sem.at[1])
    load_c = pltpu.make_async_copy(coef, cf, load_sem.at[2])
    load_s = pltpu.make_async_copy(switch, sw, load_sem.at[3])
    load_y = pltpu.make_async_copy(yf, yr, load_sem.at[4])
    load_w = [pltpu.make_async_copy(src, dst, load_sem.at[slot]) for src, dst, slot in (
        (lead_hbm, lead, 5), (chord_hbm, chord, 6), (mode_hbm, mode, 7))]
    load_p.start()
    load_x.start()

    def push(src, dst, along_x, slot, same=False):
        me, parts = (mx, xparts) if along_x else (my, yparts)

        for span in far_first(parts):
            peer = moved(me, span, parts)
            pltpu.make_async_remote_copy(
                src_ref=src if same else src.at[peer],
                dst_ref=dst.at[me],
                send_sem=push_send.at[slot],
                recv_sem=push_recv.at[slot],
                device_id=(peer, my) if along_x else (mx, peer),
                device_id_type=MESH,
            ).start()

    def arrived(dst, slot):
        part = dst.at[pl.ds(0, dst.shape[0] - 1)]
        pltpu.make_async_copy(part, part, push_recv.at[slot]).wait()

    def drained(src, slot):
        part = src.at[pl.ds(0, src.shape[0] - 1)]
        pltpu.make_async_copy(part, part, push_send.at[slot]).wait()

    def at(ref, index, rows):
        return ref[pl.ds(pl.multiple_of(index * rows, 8), rows), :]

    def put(ref, index, rows, value):
        ref[pl.ds(pl.multiple_of(index * rows, 8), rows), :] = value

    def pack(dst, member, value, rows):
        total = value.shape[0]
        strip[0:total, :] = value
        for s in range(total // rows):
            dst[s, member] = strip[s * rows:(s + 1) * rows, :]

    row = lax.broadcasted_iota(jnp.int32, (J, Z), 0)
    lane = lax.broadcasted_iota(jnp.int32, (J, Z), 1)
    row8 = lax.broadcasted_iota(jnp.int32, (8, Z), 0)

    zero_line = jnp.zeros((J, Z), F32)
    pl.semaphore_wait(barrier, nx + ny - 2)

    def neighbour(src, dst, slot, device):
        return pltpu.make_async_remote_copy(
            src_ref=src, dst_ref=dst, send_sem=halo_send.at[slot], recv_sem=halo_recv.at[slot],
            device_id=device, device_id_type=MESH)

    left, right = lax.rem(mx + nx - 1, nx), lax.rem(mx + 1, nx)
    down, up = lax.rem(my + ny - 1, ny), lax.rem(my + 1, ny)
    halos = (
        neighbour(pot.at[pl.ds((I - 2) * J, 2 * J), :], halo_prev, 0, (right, my)),
        neighbour(pot.at[pl.ds(0, J), :], halo_next, 1, (left, my)),
        neighbour(face_hi, halo_lo, 2, (mx, up)),
        neighbour(face_lo, halo_hi, 3, (mx, down)),
    )
    for halo in halos[:2]:
        halo.start()
    p[0:J, :] = zero_line
    p[J:2 * J, :] = zero_line
    p[(I + 2) * J:(I + 3) * J, :] = zero_line
    load_p.wait()
    face_hi[...] = p[pl.ds(2 * J + J - 1, I, stride=J), :]
    face_lo[...] = p[pl.ds(2 * J, I, stride=J), :]
    for halo in halos[2:]:
        halo.start()
    for load in [load_c, load_s, load_y] + load_w:
        load.start()

    pair = lax.broadcasted_iota(jnp.int32, (I, Z), 1) // 2

    def pick(value, j, kept):
        return jnp.where(pair == j, pltpu.roll(value, lax.rem(2 * j + Z // 2 + 1, Z), 1), kept)

    def planes(upper, lower):
        turned = jnp.transpose(jnp.concatenate([upper, lower], axis=0))
        return turned[Z // 2 - 1:Z // 2 + 1]

    load_x.wait()

    def gain_forward(c, gain):
        for u in range(U):
            i = c * U + u
            ratio = at(xr, i, J)
            put(xq, i, J, 0.25 * complement(ratio))
            gain = ratio * gain
            put(xg, i, J, gain)
        return gain

    x_gain = lax.fori_loop(0, I // U, gain_forward, jnp.ones((J, Z), F32))

    def gain_backward(c, carry):
        gain, cross = carry
        for u in range(U):
            i = I - 1 - (c * U + u)
            ratio = at(xr, I + i, J)
            scale = complement(ratio)
            put(xs, i, J, scale)
            gain = ratio * gain
            cross = ratio * cross + scale * at(xg, i, J)
            tg[pl.ds(i, J, stride=I), :] = gain
            tc[pl.ds(i, J, stride=I), :] = cross
        return gain, cross

    x_back, x_cross = lax.fori_loop(
        0, I // U, gain_backward, (jnp.ones((J, Z), F32), jnp.zeros((J, Z), F32)))
    pack(xgs, 0, x_gain, xrow)
    pack(xgs, 1, x_back, xrow)
    pack(xgs, 2, x_cross, xrow)

    push(xgs, xgr, True, 0)

    load_c.wait()
    load_s.wait()

    def forcing(c, _):
        rows = [at(p, c * 4 + d, J) for d in range(7)]
        for u in range(4):
            i = c * 4 + u
            before2, before, center, after = rows[u:u + 4]
            twice = center + center
            second = jnp.where(at(sw, i, J) == 1, (center - 2.0 * before) + before2,
                               (after - twice) + before)
            span = jnp.where(row == 0, 0.0, pltpu.roll(center, 1, 0)) + jnp.where(
                row == J - 1, 0.0, pltpu.roll(center, J - 1, 0))
            normal = jnp.where(lane == 0, 0.0, pltpu.roll(center, 1, 1)) + jnp.where(
                lane == Z - 1, 0.0, pltpu.roll(center, Z - 1, 1))
            residual = at(cf, i, J) * second + (span - twice) + (normal - twice)
            put(xo, i, J, at(xq, i, J) * residual)
        return 0

    lax.fori_loop(0, I // 4, forcing, 0)

    for halo in halos:
        halo.wait_recv()

    before = jnp.where(mx == 0, 0.0, halo_prev[J:2 * J, :])
    before2 = jnp.where(mx == 0, 0.0, halo_prev[0:J, :])
    after = jnp.where(mx == nx - 1, 0.0, halo_next[...])
    first = jnp.where(at(sw, 0, J) == 1, before2 - 2.0 * before, before)
    second = jnp.where(at(sw, 1, J) == 1, before, 0.0)
    last = jnp.where(at(sw, I - 1, J) == 1, 0.0, after)
    for i, term in ((0, first), (1, second), (I - 1, last)):
        put(xo, i, J, at(xo, i, J) + at(xq, i, J) * (at(cf, i, J) * term))
    low = jnp.logical_and(row8 == 0, my > 0)
    high = jnp.logical_and(row8 == 7, my < ny - 1)

    def sweep_forward(c, carry):
        head, body, tail = carry
        low8 = at(halo_lo, c, U)
        high8 = at(halo_hi, c, U)
        for u in range(U):
            base = pl.multiple_of((c * U + u) * J, 8)
            r = xr[pl.ds(base, J), :]
            f = xo[pl.ds(base, J), :]
            q0 = xq[pl.ds(base, 8), :]
            q3 = xq[pl.ds(base + J - 8, 8), :]
            head = r[0:8] * head + (f[0:8] + q0 * jnp.where(low, low8[u:u + 1], 0.0))
            body = r[8:J - 8] * body + f[8:J - 8]
            tail = r[J - 8:] * tail + (f[J - 8:] + q3 * jnp.where(high, high8[u:u + 1], 0.0))
            xo[pl.ds(base, 8), :] = head
            xo[pl.ds(base + 8, J - 16), :] = body
            xo[pl.ds(base + J - 8, 8), :] = tail
        return head, body, tail

    head, body, tail = lax.fori_loop(
        0, I // U, sweep_forward,
        (jnp.zeros((8, Z), F32), jnp.zeros((J - 16, Z), F32), jnp.zeros((8, Z), F32)))

    def sweep_backward(c, state):
        for u in range(U):
            i = I - 1 - (c * U + u)
            state = at(xr, I + i, J) * state + at(xs, i, J) * at(xo, i, J)
            to[pl.ds(i, J, stride=I), :] = state
        return state

    x_first = lax.fori_loop(0, I // U, sweep_backward, jnp.zeros((J, Z), F32))
    pack(xos, 0, jnp.concatenate([head, body, tail], axis=0), xrow)
    pack(xos, 1, x_first, xrow)
    push(xos, xor_, True, 1)

    load_y.wait()

    def span_forward(c, gain):
        for u in range(2):
            j = c * 2 + u
            ratio = yr[pl.ds(j, I, stride=J), :]
            scale = complement(ratio)
            put(yr0, j, I, ratio)
            put(tg, j, I, scale * at(tg, j, I))
            put(tc, j, I, scale * at(tc, j, I))
            put(to, j, I, scale * at(to, j, I))
            gain = ratio * gain
            put(ysc, j, I, gain)
        return gain

    y_gain = lax.fori_loop(0, J // 2, span_forward, jnp.ones((I, Z), F32))

    def chain(gains, sums, gr, sr, answers, mine, me, n, rows):
        gr[me] = gains[me]
        sr[me] = sums[me]
        state = jnp.zeros((rows, Z), F32)
        partial = []
        for k in range(n):
            answers[k, 0] = state
            partial.append(sr[k, 1] + gr[k, 2] * state)
            state = sr[k, 0] + gr[k, 0] * state
        state = jnp.zeros((rows, Z), F32)
        for k in reversed(range(n)):
            answers[k, 1] = state
            state = partial[k] + gr[k, 1] * state
        mine[me] = answers[me]

    arrived(xgr, 0)
    arrived(xor_, 1)
    chain(xgs, xos, xgr, xor_, xas, xar, mx, nx, xrow)
    push(xas, xar, True, 2)

    def span_backward(c, carry):
        gain, cross, gains2, crosses2 = carry
        for u in range(2):
            j = J - 1 - (c * 2 + u)
            ratio = yr[pl.ds(I * J + j, I, stride=J), :]
            scale = complement(ratio)
            put(yr1, j, I, ratio)
            put(ys1, j, I, scale)
            gain = ratio * gain
            cross = ratio * cross + scale * at(ysc, j, I)
            put(ygb, j, I, gain)
            put(ycc, j, I, cross)
            gains2 = pick(gain, j, gains2)
            crosses2 = pick(cross, j, crosses2)
        return gain, cross, gains2, crosses2

    zero_face = jnp.zeros((I, Z), F32)
    y_back, y_cross, gains2, crosses2 = lax.fori_loop(
        0, J // 2, span_backward, (jnp.ones((I, Z), F32), zero_face, zero_face, zero_face))
    wide[0:I, :] = gains2
    wide[I:2 * I, :] = crosses2
    pack(ygs, 0, y_gain, yrow)
    pack(ygs, 1, y_back, yrow)
    pack(ygs, 2, y_cross, yrow)
    push(ygs, ygr, False, 3)
    mgs[0] = planes(y_gain, y_back)
    mgs[1] = planes(y_cross, y_cross)
    push(mgs, mgr, False, 7, True)

    arrived(xar, 2)

    def across(c, state):
        for u in range(4 * xrow):
            s, t = c * 4 + u // xrow, u % xrow
            j = c * 4 * xrow + u
            a = xar[s, 0, t:t + 1, :]
            b = xar[s, 1, t:t + 1, :]
            source = at(to, j, I) + at(tg, j, I) * b + at(tc, j, I) * a
            state = at(yr0, j, I) * state + source
            put(yfw, j, I, state)
        return state

    y_last = lax.fori_loop(0, nx // 4, across, jnp.zeros((I, Z), F32))

    def back(c, state):
        for u in range(U):
            j = J - 1 - (c * U + u)
            state = at(yr1, j, I) * state + at(ys1, j, I) * at(yfw, j, I)
            put(ycb, j, I, state)
        return state

    y_first = lax.fori_loop(0, J // U, back, jnp.zeros((I, Z), F32))
    pack(yos, 0, y_last, yrow)
    pack(yos, 1, y_first, yrow)
    push(yos, yor, False, 4)
    mos[...] = planes(y_last, y_first)
    push(mos, mor, False, 8, True)


    def own_planes(j, kept):
        return pick(p[pl.ds(2 * J + j, I, stride=J), :] + at(ycb, j, I), j, kept)

    jump = lax.fori_loop(0, J, own_planes, zero_face)

    for load in load_w:
        load.wait()
    stream = mx * I + lax.broadcasted_iota(jnp.int32, (J, I), 1)
    begin = jnp.transpose(jnp.broadcast_to(lead[...], (8, J)))[:, 0:1]
    length = jnp.transpose(jnp.broadcast_to(chord[...], (8, J)))[:, 0:1]
    onwing = jnp.logical_and(stream >= begin, stream < begin + length)
    weight = jnp.where(onwing, 0.5 + 2.5 * stream.astype(F32) / (I * nx), 0.0) / jnp.sqrt(
        length.astype(F32))
    weights = []
    for m in range(MODES):
        own = jnp.concatenate(
            [jnp.where(mode[...] == m, weight, 0.0), jnp.zeros((J, Z - I), F32)], axis=1)
        rows = 2 * I + m * 2 * J
        wide[pl.ds(rows, J, stride=2), :] = -own
        wide[pl.ds(rows + 1, J, stride=2), :] = own
        weights.append(jnp.transpose(wide[rows:rows + 2 * J, :])[0:I])

    arrived(ygr, 3)
    arrived(yor, 4)
    chain(ygs, yos, ygr, yor, yas, yar, my, ny, yrow)
    push(yas, yar, False, 5)

    arrived(mgr, 7)
    arrived(mor, 8)
    mgr[my] = mgs[...]
    mor[my] = mos[...]
    state = jnp.zeros((2, Z), F32)
    from_left = from_right = state
    partial = []
    for k in range(ny):
        from_left = jnp.where(my == k, state, from_left)
        partial.append(mor[k] + mgr[k, 1] * pltpu.roll(state, I, 1))
        state = mor[k] + mgr[k, 0] * state
    state = jnp.zeros((2, Z), F32)
    for k in reversed(range(ny)):
        from_right = jnp.where(my == k, state, from_right)
        state = partial[k] + mgr[k, 0] * state
    lanes = lax.broadcasted_iota(jnp.int32, (2, Z), 1)
    states = jnp.concatenate(
        [jnp.where(lanes < I, from_left, from_right), jnp.zeros((6, Z), F32)], axis=0)
    states = jnp.transpose(states)
    odd = lax.rem(lax.broadcasted_iota(jnp.int32, (I, Z), 1), 2) == 1
    left_state = jnp.where(odd, states[0:I, 1:2], states[0:I, 0:1])
    right_state = jnp.where(odd, states[I:2 * I, 1:2], states[I:2 * I, 0:1])
    jump = jump + wide[0:I, :] * right_state + wide[I:2 * I, :] * left_state
    for m in range(MODES):
        ls[m:m + 1, 0:2 * J] = jnp.sum(weights[m] * jump[:, 0:2 * J], axis=0, keepdims=True)

    ls[:, 2 * J:] = jnp.zeros((MODES, Z - 2 * J), F32)
    push(ls, lr, True, 6, True)
    lr[mx] = ls[...]

    arrived(lr, 6)
    total = lr[0]
    for k in range(1, nx):
        total = total + lr[k]
    fold = lax.broadcasted_iota(jnp.int32, (Z, J), 0) // 2 == lax.broadcasted_iota(
        jnp.int32, (Z, J), 1)
    loads[...] = jnp.dot(total, fold.astype(F32), precision=lax.Precision.HIGHEST,
                         preferred_element_type=F32)

    arrived(yar, 5)
    for halo in halos:
        halo.wait_send()
    for src, slot in ((xgs, 0), (xos, 1), (xas, 2), (ygs, 3), (yos, 4), (yas, 5), (lr, 6), (mgr, 7),
                      (mor, 8)):
        drained(src, slot)


def finish(I, J, Z, own, from_right, from_left, states, sums, out, loads, ya, yb, rows, sem):
    ny, _, yrow, _ = states.shape
    copies = [pltpu.make_async_copy(sums, loads, sem.at[0])]
    copies[0].start()
    for c in range(I // 8):
        for s in range(c * 8 // yrow, (c + 1) * 8 // yrow):
            ya[s * yrow:(s + 1) * yrow, :] = states[s, 0]
            yb[s * yrow:(s + 1) * yrow, :] = states[s, 1]
        a = ya[8 * c:8 * c + 8, :]
        b = yb[8 * c:8 * c + 8, :]
        for j in range(J):
            part = pl.ds(j * I + 8 * c, 8)
            rows[pl.ds(8 * c * J + j, 8, stride=J), :] = (
                own[part, :] + from_right[part, :] * b + from_left[part, :] * a)
        cells = pl.ds(8 * c * J, 8 * J)
        copies.append(pltpu.make_async_copy(rows.at[cells, :], out.at[cells, :], sem.at[c + 1]))
        copies[-1].start()
    for copy in copies:
        copy.wait()


def shards(nx, ny, potential, coefficient, shock_switch, x_factors, y_factors, wing_lead, wing_chord,
           panel_mode):
    I, J, Z = potential.shape
    cells = I * J
    xrow, yrow = J // nx, I // ny
    any_space = pl.BlockSpec(memory_space=pl.ANY)
    vmem = pl.BlockSpec(memory_space=pltpu.VMEM)
    block = pltpu.VMEM((cells, Z), F32)
    face = pltpu.VMEM((I, Z), F32)
    scratch = [
        pltpu.VMEM((cells + 3 * J, Z), F32),
        block,
        pltpu.VMEM((cells, Z), jnp.int32),
        pltpu.VMEM((2 * cells, Z), F32),
        pltpu.VMEM((2 * cells, Z), F32),
    ] + [block] * 12 + [face] * 4 + [
        pltpu.VMEM((2 * J, Z), F32),
        pltpu.VMEM((J, Z), F32),
        face,
    ]
    for n, rows in ((nx, xrow), (ny, yrow)):
        for members in (3, 2, 2):
            scratch += [pltpu.VMEM((n, members, rows, Z), F32)] * 2
    scratch.pop()
    scratch += [
        pltpu.VMEM((MODES, Z), F32),
        pltpu.VMEM((nx, MODES, Z), F32),
        pltpu.VMEM((2, 2, Z), F32),
        pltpu.VMEM((ny, 2, 2, Z), F32),
        pltpu.VMEM((2, Z), F32),
        pltpu.VMEM((ny, 2, Z), F32),
        pltpu.VMEM((2 * I + 2 * J * MODES, Z), F32),
        pltpu.VMEM((1, J), jnp.int32),
        pltpu.VMEM((1, J), jnp.int32),
        pltpu.VMEM((J, I), jnp.int32),
        pltpu.SemaphoreType.DMA((8,)),
        pltpu.SemaphoreType.DMA((4,)),
        pltpu.SemaphoreType.DMA((4,)),
        pltpu.SemaphoreType.DMA((9,)),
        pltpu.SemaphoreType.DMA((9,)),
    ]
    own, from_right, from_left, states, sums = pl.pallas_call(
        functools.partial(kernel, nx, ny, I, J, Z),
        out_shape=(
            block,
            block,
            block,
            pltpu.VMEM((ny, 2, yrow, Z), F32),
            pltpu.VMEM((MODES, J), F32),
        ),
        in_specs=[any_space] * 8,
        out_specs=(vmem,) * 5,
        scratch_shapes=scratch,
        compiler_params=pltpu.CompilerParams(
            collective_id=0, has_side_effects=True, vmem_limit_bytes=60 * 1024 * 1024),
        name="factored_step",
    )(
        potential.reshape(cells, Z),
        coefficient.reshape(cells, Z),
        shock_switch.reshape(cells, Z),
        x_factors.reshape(2 * cells, Z),
        y_factors.reshape(2 * cells, Z),
        wing_lead.reshape(1, J),
        wing_chord.reshape(1, J),
        panel_mode.T,
    )
    correction, loads = pl.pallas_call(
        functools.partial(finish, I, J, Z),
        out_shape=(
            jax.ShapeDtypeStruct((cells, Z), F32),
            jax.ShapeDtypeStruct((MODES, J), F32),
        ),
        in_specs=[vmem] * 5,
        out_specs=(any_space, any_space),
        scratch_shapes=[face, face, block, pltpu.SemaphoreType.DMA((I // 8 + 1,))],
        compiler_params=pltpu.CompilerParams(vmem_limit_bytes=4 * 1024 * 1024),
        name="finish",
    )(own, from_right, from_left, states, sums)
    return correction.reshape(I, J, Z), loads


def solution(mesh):
    placed = (
        P("gx", "gy", None),
        P("gx", "gy", None),
        P("gx", "gy", None),
        P(None, "gx", "gy", None),
        P(None, "gx", "gy", None),
        P("gy"),
        P("gy"),
        P("gx", "gy"),
    )
    return jax.shard_map(
        functools.partial(shards, mesh.shape["gx"], mesh.shape["gy"]),
        mesh=mesh,
        in_specs=placed,
        out_specs=(P("gx", "gy", None), P(None, "gy")),
        check_vma=False,
    )
```
